512 devices in a mesh: blk: 128 (over y_hi, x, z), feat: 4 (over y_lo, core).
Axes of the slice: x: 4, y: 4 (y_hi: 2, y_lo: 2; y = y_hi * 2 + y_lo), z: 16, core: 2. Of those that a mesh axis runs over, the one named last changes fastest.
Arguments:
- points: bfloat16 [16384, 8192], P('blk', 'feat'), may hold values from -12 to 12
- centers: bfloat16 [2048, 8192], P('blk', 'feat'), may hold values from -12 to 12
- coefs: bfloat16 [2048, 1024], P('blk', 'feat'), may hold values from -16 to 16
Outputs:
- normal_prod: float32 [2048, 1024], P('blk', 'feat')
The draws below stay inside these ranges and needn't reach their ends.
All inputs are finite; a program needn't handle non-finite values.
Results may differ from the reference program's by a relative error of at most 0.0011.
Values may be sent and summed in bfloat16 or wider, within the bound.
A program may use at most 64 MiB of HBM per device.

```python
import math
import jax
import jax.numpy as jnp
from jax import lax

F = 8192
L = 1024
NPTS = 16384
M = 2048


def field_law():
    return (16, 1.0, 2.0, 0.8, 0.97)


def mixed_rows(key, row_total, salt_id):
    latent_dims, latent_var, resid_var, mix_low, mix_high = field_law()
    basis_rows = jax.random.normal(jax.random.fold_in(key, 101), (latent_dims, F), jnp.float32)
    latent = jax.random.normal(jax.random.fold_in(key, salt_id), (row_total, latent_dims), jnp.float32)
    latent = latent * jnp.sqrt(latent_var / latent_dims)
    residual = jax.random.normal(jax.random.fold_in(key, salt_id + 1), (row_total, F), jnp.float32)
    residual = residual * jnp.sqrt(resid_var)
    return jnp.dot(latent, basis_rows, precision=lax.Precision.HIGHEST) + residual


def draw_centers(key, part):
    return jnp.clip(mixed_rows(key, M, 3), -12.0, 12.0).astype(jnp.bfloat16)


def draw_points(key, part):
    latent_dims, latent_var, resid_var, mix_low, mix_high = field_law()
    anchors = mixed_rows(key, M, 3)
    fresh_rows = mixed_rows(key, NPTS, 1)
    owner_row = jax.random.randint(jax.random.fold_in(key, 7), (NPTS,), 0, M)
    mix_weight = jax.random.uniform(jax.random.fold_in(key, 9), (NPTS, 1), jnp.float32, mix_low, mix_high)
    mixed = mix_weight * jnp.take(anchors, owner_row, axis=0) + jnp.sqrt(1.0 - mix_weight * mix_weight) * fresh_rows
    return jnp.clip(mixed, -12.0, 12.0).astype(jnp.bfloat16)


def levels(own_key, shape, pieces, low, largest):
    level = 1.0
    for axis_at, parts in pieces:
        heights = jax.random.uniform(jax.random.fold_in(jax.random.fold_in(own_key, 6), axis_at), (parts,), jnp.float32, low / len(pieces), largest / len(pieces))
        level = level * jnp.repeat(jnp.exp(heights), shape[axis_at] // parts).reshape((-1,) + (1,) * (len(shape) - 1 - axis_at))
    return level


def scatter_about(key, dims, spread, most, split=(), kind=jnp.bfloat16):
    result = spread * jax.random.normal(key, dims, jnp.float32)
    if split:
        result = result * levels(key, dims, split, -0.22, 0.18)
    return jnp.clip(result, -most, most).astype(kind)


def setup_inputs(seed: int = 0) -> dict:
    splits = jax.random.split(jax.random.key(seed), 4)
    points = draw_points(jax.random.fold_in(splits[3], 71), 0)
    centers = draw_centers(jax.random.fold_in(splits[3], 71), 0)
    coefs = scatter_about(splits[2], (M, L), 2.5, 16.0, ((0, 128), (1, 4)))
    return {"points": points, "centers": centers, "coefs": coefs}


def reference(points, centers, coefs):
    point_sq = jnp.einsum('nf,nf->n', points, points, preferred_element_type=jnp.float32)
    center_sq = jnp.einsum('mf,mf->m', centers, centers, preferred_element_type=jnp.float32)
    cross_dot = lax.dot_general(points, centers, (((1,), (1,)), ((), ())), preferred_element_type=jnp.float32)
    dist = point_sq[:, None] + center_sq[None, :] - 2.0 * cross_dot
    kernel = jnp.exp(-dist / F).astype(jnp.bfloat16)
    fitted = jnp.dot(kernel, coefs, preferred_element_type=jnp.float32).astype(jnp.bfloat16)
    summed = lax.dot_general(kernel, fitted, (((0,), (0,)), ((), ())), preferred_element_type=jnp.float32)
    return summed * (1.0 / math.sqrt(NPTS))
```

```python
import functools
import math

import jax
import jax.numpy as jnp
from jax import lax
from jax.experimental import pallas as pl
from jax.experimental.pallas import tpu as pltpu
from jax.sharding import PartitionSpec as P

MESH = pl.DeviceIdType.MESH
F32, BF16 = jnp.float32, jnp.bfloat16
NX, NY, NZ = 4, 4, 16
COPIES = 160


def kernel(
    inv_f, scale, pts, ctr, wts, out,
    px, cx, wx, dsend, dcore, dsum, r1a, r1b, r2a, r2b, kx,
    gsend, gcore, gsum, g1a, g1b, g2a, g2b, gout, zb,
    ssem, rsem, lsem,
):
    b, q = lax.axis_index("blk"), lax.axis_index("feat")
    yh, x, z = b // (NX * NZ), (b // NZ) % NX, b % NZ
    yl, c = q // 2, q % 2
    y = 2 * yh + yl
    rows, feats = pts.shape[0], pts.shape[1] // 2
    crow = ctr.shape[0]
    cblk = NZ * crow
    labels = wts.shape[1]

    def dev(yh_=None, x_=None, z_=None, q_=None):
        yh_ = yh if yh_ is None else yh_
        x_ = x if x_ is None else x_
        z_ = z if z_ is None else z_
        return ((yh_ * NX + x_) * NZ + z_, q if q_ is None else q_)

    def ydev(y_):
        return dev(yh_=y_ // 2, q_=(y_ % 2) * 2 + c)

    xp, xm, x2 = (x + 1) % NX, (x + 3) % NX, (x + 2) % NX
    yp, ym, y2 = (y + 1) % NY, (y + 3) % NY, (y + 2) % NY
    d_xp, d_xm, d_x2 = dev(x_=xp), dev(x_=xm), dev(x_=x2)
    d_zp, d_zm = dev(z_=(z + 1) % NZ), dev(z_=(z + NZ - 1) % NZ)
    d_yp, d_ym, d_y2 = ydev(yp), ydev(ym), ydev(y2)
    d_sib = dev(q_=2 * yl + 1 - c)
    d_tr = dev(x_=q, q_=x)
    diag = x == q

    used = [0]

    def new(n=1):
        used[0] += n
        assert used[0] <= COPIES
        return used[0] - n

    pending = []

    def send(i, src, dst, to):
        cp = pltpu.make_async_remote_copy(
            src_ref=src, dst_ref=dst, send_sem=ssem.at[i], recv_sem=rsem.at[i],
            device_id=to, device_id_type=MESH,
        )
        cp.start()
        pending.append(cp)

    def arrive(i, dst, frm):
        pltpu.make_async_remote_copy(
            src_ref=dst, dst_ref=dst, send_sem=ssem.at[i], recv_sem=rsem.at[i],
            device_id=frm, device_id_type=MESH,
        ).wait_recv()

    def half(ref, h):
        return ref.at[:, pl.ds(pl.multiple_of(h * feats, 128), feats)]

    def ctr_at(yh_, z_):
        return cx.at[pl.ds(pl.multiple_of(yh_ * cblk + z_ * crow, 16), crow)]

    def w_at(x_, yh_, z_):
        return wx.at[pl.ds(pl.multiple_of((2 * x_ + yh_) * cblk + z_ * crow, 16), crow)]

    def w_blk(q_, yh_, part=None):
        start, size = (2 * q_ + yh_) * cblk, cblk
        if part is not None:
            start, size = start + part * (cblk // 2), cblk // 2
        return wx.at[pl.ds(pl.multiple_of(start, 16), size)]

    loads = [
        pltpu.make_async_copy(half(ctr, yh), ctr_at(yh, z), lsem.at[0]),
        pltpu.make_async_copy(half(pts, yh), px.at[x, yh], lsem.at[1]),
    ]
    for cp in loads:
        cp.start()

    barrier = pltpu.get_barrier_semaphore()
    near = (d_zp, d_zm, d_xp, d_xm, d_x2, d_yp, d_ym, d_y2, d_sib)
    for other in near:
        pl.semaphore_signal(barrier, inc=1, device_id=other, device_id_type=MESH)

    @pl.when(jnp.logical_not(diag))
    def _():
        pl.semaphore_signal(barrier, inc=1, device_id=d_tr, device_id_type=MESH)
        pl.semaphore_wait(barrier, len(near) + 1)

    @pl.when(diag)
    def _():
        pl.semaphore_wait(barrier, len(near))

    oh = 1 - yh
    zc = [[[new() for _ in range(NZ // 2)] for _ in range(3)] for _ in range(2)]

    def z_piece(kind, zs):
        zs = (zs + NZ) % NZ
        if kind == 0:
            return ctr_at(yh, zs)
        if kind == 1:
            return ctr_at(oh, zs)
        return w_at(q, yh, zs)

    def z_last(d, kind):
        return NZ // 2 if (kind == 1) == (d == 1) else NZ // 2 - 1

    def z_send(d, kind, step, src=None):
        if step > z_last(d, kind):
            return
        sign = -1 if d == 0 else 1
        piece = z_piece(kind, z + sign * (step - 1))
        send(zc[d][kind][step - 1], piece if src is None else src, piece, d_zp if d == 0 else d_zm)

    def z_arrive(d, kind, step):
        if step > z_last(d, kind):
            return
        sign = -1 if d == 0 else 1
        arrive(zc[d][kind][step - 1], z_piece(kind, z + sign * step), d_zm if d == 0 else d_zp)

    i_sc, i_sp, i_w = new(), new(), new()
    for d in range(2):
        z_send(d, 0, 1, half(ctr, yh))
    send(i_sc, half(ctr, oh), ctr_at(yh, z), d_y2)

    @pl.when(jnp.logical_not(diag))
    def _():
        cp = pltpu.make_async_remote_copy(
            src_ref=wts, dst_ref=w_at(x, yh, z), send_sem=ssem.at[i_w], recv_sem=rsem.at[i_w],
            device_id=d_tr, device_id_type=MESH,
        )
        cp.start()

    @pl.when(diag)
    def _():
        pltpu.make_async_copy(wts, w_at(x, yh, z), lsem.at[2]).start()

    i_x = [[new(), new()] for _ in range(2)]
    i_xf = [[new(), new()] for _ in range(2)]
    hrow = rows // 2

    def x_own(j, src):
        for k, to in enumerate((d_xp, d_xm)):
            send(i_x[j][k], src, px.at[x, yh if j == 0 else oh], to)

    def x_forward(j):
        yy = yh if j == 0 else oh
        arrive(i_x[j][0], px.at[xm, yy], d_xm)
        part = px.at[xm, yy, pl.ds(0, hrow)]
        send(i_xf[j][0], part, part, d_xp)
        arrive(i_x[j][1], px.at[xp, yy], d_xp)
        part = px.at[xp, yy, pl.ds(hrow, hrow)]
        send(i_xf[j][1], part, part, d_xm)

    x_own(0, half(pts, yh))
    send(i_sp, half(pts, oh), px.at[x, yh], d_y2)

    arrive(i_sc, ctr_at(oh, z), d_y2)
    for d in range(2):
        z_send(d, 1, 1)

    @pl.when(jnp.logical_not(diag))
    def _():
        arrive(i_w, w_at(q, yh, z), d_tr)

    @pl.when(diag)
    def _():
        pltpu.make_async_copy(wts, w_at(x, yh, z), lsem.at[2]).wait()

    for d in range(2):
        z_send(d, 2, 1)

    for step in range(1, NZ // 2 + 1):
        for kind in (0, 1, 2):
            for d in range(2):
                z_arrive(d, kind, step)
                z_send(d, kind, step + 1)
        if step == 2:
            x_forward(0)
        if step == 3:
            arrive(i_sp, px.at[x, oh], d_y2)
            x_own(1, px.at[x, oh])
        if step == 5:
            x_forward(1)
    for cp in loads:
        cp.wait()

    i_wy = [new(), new()]
    i_wf = [new(), new()]
    i_ws = [new() for _ in range(5)]

    def w_y(y_, c_=c, part=None):
        return w_blk((y_ % 2) * 2 + c_, y_ // 2, part)

    send(i_wy[0], w_y(y), w_y(y), d_yp)
    send(i_wy[1], w_y(y), w_y(y), d_ym)
    send(i_ws[0], w_y(y), w_y(y), d_sib)

    cv = cx[...].astype(F32)
    csq = jnp.sum(cv * cv, axis=1, keepdims=True)
    csq = jnp.transpose(jnp.broadcast_to(csq, (csq.shape[0], 128)))[0:1, :]
    order = (x, xm, xp, x2)
    i_dc = [new() for _ in range(4)]

    def partial_dist(xs, yy):
        p = px[xs, yy]
        pf = p.astype(F32)
        psq = jnp.sum(pf * pf, axis=1, keepdims=True)
        cross = lax.dot_general(p, cx[...], (((1,), (1,)), ((), ())), preferred_element_type=F32)
        return psq + csq - 2.0 * cross

    for i, xs in enumerate(order):
        if i == 3:
            for j, yy in enumerate((yh, oh)):
                arrive(i_xf[j][0], px.at[x2, yy, pl.ds(0, hrow)], d_xm)
                arrive(i_xf[j][1], px.at[x2, yy, pl.ds(hrow, hrow)], d_xp)
        dsend[i] = partial_dist(xs, 1 - c)
        send(i_dc[i], dsend.at[i], dcore.at[i], d_sib)
        dsum[i] = partial_dist(xs, c)

    def ring(total, recv1a, recv1b, recv2a, recv2b, size, add_core, finish):
        n = len(total)
        hs = size // 2
        i1 = [[new(), new()] for _ in range(n)]
        i2 = [[new(), new()] for _ in range(n)]

        def sl(i, t, lo=0, num=size):
            return total[i](t, lo, num)

        for i in range(n):
            add_core(i)
            send(i1[i][0], sl(i, y2, 0, hs), recv1a.at[i], d_yp)
            send(i1[i][1], sl(i, y2, hs, hs), recv1b.at[i], d_ym)
        for i in range(n):
            arrive(i1[i][0], recv1a.at[i], d_ym)
            ref = sl(i, yp, 0, hs)
            ref[...] = ref[...] + recv1a[i]
            send(i2[i][0], sl(i, yp), recv2a.at[i], d_yp)
            arrive(i1[i][1], recv1b.at[i], d_yp)
            ref = sl(i, ym, hs, hs)
            ref[...] = ref[...] + recv1b[i]
            send(i2[i][1], sl(i, ym), recv2b.at[i], d_ym)
        for i in range(n):
            arrive(i2[i][0], recv2a.at[i], d_ym)
            arrive(i2[i][1], recv2b.at[i], d_yp)
            finish(i, sl(i, y)[...] + recv2a[i] + recv2b[i])

    def d_core(i):
        arrive(i_dc[i], dcore.at[i], d_sib)
        dsum[i] = dsum[i] + dcore[i]

    drow = rows // NY
    i_k = [[new() for _ in range(3)] for _ in range(4)]

    def k_at(x_, xs):
        return kx.at[x_, pl.ds(pl.multiple_of(xs * drow, 16), drow)]

    def d_finish(i, dist):
        ref = k_at(x, order[i])
        ref[...] = jnp.exp(dist * (-inv_f)).astype(BF16)
        for k, to in enumerate((d_xp, d_xm, d_x2)):
            send(i_k[i][k], ref, ref, to)

    def d_slice(i):
        return lambda t, lo, num: dsum.at[i, pl.ds(pl.multiple_of(t * drow + lo, 8), num)]

    ring([d_slice(i) for i in range(4)], r1a, r1b, r2a, r2b, drow, d_core, d_finish)

    arrive(i_wy[0], w_y(ym), d_ym)
    send(i_wf[0], w_y(ym, part=0), w_y(ym, part=0), d_yp)
    send(i_ws[1], w_y(ym), w_y(ym), d_sib)
    arrive(i_wy[1], w_y(yp), d_yp)
    send(i_wf[1], w_y(yp, part=1), w_y(yp, part=1), d_ym)
    send(i_ws[2], w_y(yp), w_y(yp), d_sib)
    arrive(i_wf[0], w_y(y2, part=0), d_ym)
    send(i_ws[3], w_y(y2, part=0), w_y(y2, part=0), d_sib)
    arrive(i_wf[1], w_y(y2, part=1), d_yp)
    send(i_ws[4], w_y(y2, part=1), w_y(y2, part=1), d_sib)
    arrive(i_ws[0], w_y(y, 1 - c), d_sib)
    arrive(i_ws[1], w_y(ym, 1 - c), d_sib)
    arrive(i_ws[2], w_y(yp, 1 - c), d_sib)
    arrive(i_ws[3], w_y(y2, 1 - c, 0), d_sib)
    arrive(i_ws[4], w_y(y2, 1 - c, 1), d_sib)

    shift = (0, 3, 1, 2)
    for i in range(4):
        for k, (xs, frm) in enumerate(((xm, d_xm), (xp, d_xp), (x2, d_x2))):
            arrive(i_k[i][k], k_at(xs, (xs + shift[i]) % NX), frm)

    fit = jnp.dot(kx[0], wx[0 : 2 * cblk], preferred_element_type=F32)
    for xs in range(1, NX):
        fit = fit + jnp.dot(
            kx[xs], wx[2 * xs * cblk : 2 * (xs + 1) * cblk], preferred_element_type=F32
        )
    fit = fit.astype(BF16)

    def contrib(y_, c_):
        kk = kx[(y_ % 2) * 2 + c_, :, pl.ds(pl.multiple_of((y_ // 2) * cblk, 128), cblk)]
        return lax.dot_general(kk, fit, (((0,), (0,)), ((), ())), preferred_element_type=F32)

    i_gc = [new() for _ in range(4)]
    gorder = (y2, yp, ym, y)
    for i, y_ in enumerate(gorder):
        gsend[i] = contrib(y_, 1 - c)
        send(i_gc[i], gsend.at[i], gcore.at[i], d_sib)
    for i, y_ in enumerate(gorder):
        gsum[y_] = contrib(y_, c)
    for i, y_ in enumerate(gorder):
        arrive(i_gc[i], gcore.at[i], d_sib)
        gsum[y_] = gsum[y_] + gcore[i]

    grow = cblk // 4
    zper = grow // crow
    i_z = new(NZ)
    zpart = [(z // zper + s) % 4 for s in (2, 1, 3, 0)]

    def g_slice(i):
        return lambda t, lo, num: gsum.at[t, pl.ds(pl.multiple_of(zpart[i] * grow + lo, 8), num)]

    def z_copy(zs, to, slot):
        return pltpu.make_async_remote_copy(
            src_ref=gout.at[pl.ds(pl.multiple_of(zs * crow, 16), crow)], dst_ref=zb.at[slot],
            send_sem=ssem.at[i_z + zs], recv_sem=rsem.at[i_z + slot],
            device_id=to, device_id_type=MESH,
        )

    def g_finish(i, val):
        gout[pl.ds(pl.multiple_of(zpart[i] * grow, 16), grow)] = val
        for j in range(zper):
            zs = zpart[i] * zper + j
            own = jnp.logical_and(diag, zs == z)

            @pl.when(jnp.logical_not(own))
            def _():
                z_copy(zs, dev(x_=q, z_=zs, q_=x), z).start()

            @pl.when(own)
            def _():
                zb[z] = val[j * crow : (j + 1) * crow]

    ring([g_slice(i) for i in range(4)], g1a, g1b, g2a, g2b, grow, lambda i: None, g_finish)

    total = None
    for s in range(NZ):
        @pl.when(jnp.logical_not(jnp.logical_and(diag, z == s)))
        def _():
            z_copy(s, dev(x_=q, z_=s, q_=x), s).wait_recv()
    for s in range(NZ):
        total = zb[s] if total is None else total + zb[s]
    out[...] = total * scale

    for cp in pending:
        cp.wait_send()

    @pl.when(jnp.logical_not(diag))
    def _():
        pltpu.make_async_remote_copy(
            src_ref=wts, dst_ref=w_at(x, yh, z), send_sem=ssem.at[i_w], recv_sem=rsem.at[i_w],
            device_id=d_tr, device_id_type=MESH,
        ).wait_send()

    for s in range(NZ):
        @pl.when(jnp.logical_not(jnp.logical_and(diag, z == s)))
        def _():
            z_copy(s, dev(x_=q, z_=s, q_=x), s).wait_send()


def solution(mesh):
    assert mesh.shape["blk"] == 2 * NX * NZ and mesh.shape["feat"] == 4

    def step(points, centers, coefs):
        rows, qf = points.shape
        crow, labels = coefs.shape
        feats, cblk = qf // 2, NZ * crow
        npts = rows * mesh.shape["blk"]
        nf = qf * mesh.shape["feat"]
        drow, grow = rows // NY, cblk // 4
        V = pltpu.VMEM
        return pl.pallas_call(
            functools.partial(kernel, 1.0 / nf, 1.0 / math.sqrt(npts)),
            out_shape=jax.ShapeDtypeStruct((crow, labels), F32),
            in_specs=[pl.BlockSpec(memory_space=pl.ANY)] * 3,
            out_specs=pl.BlockSpec(memory_space=pltpu.VMEM),
            scratch_shapes=[
                V((NX, 2, rows, feats), BF16),
                V((2 * cblk, feats), BF16),
                V((2 * NX * cblk, labels), BF16),
                V((4, rows, 2 * cblk), F32),
                V((4, rows, 2 * cblk), F32),
                V((4, rows, 2 * cblk), F32),
                V((4, drow // 2, 2 * cblk), F32),
                V((4, drow // 2, 2 * cblk), F32),
                V((4, drow, 2 * cblk), F32),
                V((4, drow, 2 * cblk), F32),
                V((NX, rows, 2 * cblk), BF16),
                V((4, cblk, labels), F32),
                V((4, cblk, labels), F32),
                V((4, cblk, labels), F32),
                V((4, grow // 2, labels), F32),
                V((4, grow // 2, labels), F32),
                V((4, grow, labels), F32),
                V((4, grow, labels), F32),
                V((cblk, labels), F32),
                V((NZ, crow, labels), F32),
                pltpu.SemaphoreType.DMA((COPIES,)),
                pltpu.SemaphoreType.DMA((COPIES,)),
                pltpu.SemaphoreType.DMA((3,)),
            ],
            compiler_params=pltpu.CompilerParams(
                collective_id=0, has_side_effects=True, vmem_limit_bytes=48 << 20
            ),
        )(points, centers, coefs)

    spec = P("blk", "feat")
    return jax.shard_map(
        step, mesh=mesh, in_specs=(spec, spec, spec), out_specs=spec, check_vma=False
    )
```

```python
import functools
import math

import jax
import jax.numpy as jnp
from jax import lax
from jax.experimental import pallas as pl
from jax.experimental.pallas import tpu as pltpu
from jax.sharding import PartitionSpec as P

MESH = pl.DeviceIdType.MESH
F32, BF16 = jnp.float32, jnp.bfloat16
NX, NY, NZ = 4, 4, 16
SENDS, ARRIVALS = 24, 64
REL = [0] + [s * d for d in range(1, NZ // 2) for s in (1, -1)] + [NZ // 2]
REL.remove(4), REL.insert(7, 4)
SLOT = {r: i for i, r in enumerate(REL)}
HALF = NZ // 2
OWN, LEFT, RIGHT, FAR = range(4)
UNITS = ((OWN, 0), (OWN, 1), (LEFT, 0), (RIGHT, 1), (LEFT, 1), (RIGHT, 0), (FAR, 0), (FAR, 1))
UNIT = {u: i for i, u in enumerate(UNITS)}
PIECES = ((0, 2, 0), (2, 4, 0), (4, 8, 0), (0, 4, 1), (4, 8, 1))
NEAR = [0, 1, -1, 2, -2, 3, -3, 4, -4]
NP = len(PIECES)


def kernel(
    inv_f, scale, pts, ctr, wts, out,
    px, cx, wx, kx, gsum, gout, zb, *rest,
):
    g1, g2, za, psq, fitted = rest[:5]
    dpart, dcore, r1, r2 = (rest[5 + NP * i : 5 + NP * (i + 1)] for i in range(4))
    ssem, rsem, lsem = rest[5 + 4 * NP :]
    b, q = lax.axis_index("blk"), lax.axis_index("feat")
    yh, x, z = b // (NX * NZ), (b // NZ) % NX, b % NZ
    yl, c = q // 2, q % 2
    y, oh = 2 * yh + yl, 1 - yh
    feats = pts.shape[1] // 2
    hrow = pts.shape[0] // 2
    crow = ctr.shape[0]
    cset = 2 * HALF * crow
    lab = wts.shape[1] // 2

    def dev(yh_=None, x_=None, z_=None, q_=None):
        yh_ = yh if yh_ is None else yh_
        x_ = x if x_ is None else x_
        z_ = z if z_ is None else z_
        return ((yh_ * NX + x_) * NZ + z_, q if q_ is None else q_)

    def ydev(y_):
        return dev(yh_=y_ // 2, q_=(y_ % 2) * 2 + c)

    def zat(rel):
        return (z + rel + NZ) % NZ

    xp, xm, x2 = (x + 1) % NX, (x + 3) % NX, (x + 2) % NX
    xabs = (x, xm, xp, x2)
    yp, ym, y2 = (y + 1) % NY, (y + 3) % NY, (y + 2) % NY
    d_xp, d_xm, d_x2 = dev(x_=xp), dev(x_=xm), dev(x_=x2)
    d_yp, d_ym, d_y2 = ydev(yp), ydev(ym), ydev(y2)
    d_sib = dev(q_=2 * yl + 1 - c)
    diag = x == q

    used = [0, 0]

    def counter(which, limit):
        def new():
            used[which] += 1
            assert used[which] <= limit
            return used[which] - 1
        return new

    new_s, new = counter(0, SENDS), counter(1, ARRIVALS)

    def copy(o, i, src, dst, to):
        return pltpu.make_async_remote_copy(
            src_ref=src, dst_ref=dst, send_sem=ssem.at[o], recv_sem=rsem.at[i],
            device_id=to, device_id_type=MESH,
        )

    def send(o, i, src, dst, to):
        copy(o, i, src, dst, to).start()

    def arrive(i, ref):
        copy(0, i, ref, ref, d_sib).wait_recv()

    def sent(o, ref):
        copy(o, 0, ref, ref, d_sib).wait_send()

    def half(ref, h, lo=0, num=None):
        num = ref.shape[0] if num is None else num
        return ref.at[pl.ds(lo, num), pl.ds(pl.multiple_of(h * feats, 128), feats)]

    def ctr_at(yh_, rel):
        return cx.at[SLOT[HALF if rel == -HALF else rel], yh_]

    def z_piece(kind, rel):
        if kind == 2:
            return wx.at[SLOT[HALF if rel == -HALF else rel]]
        return ctr_at(oh if kind == 1 else yh, rel)

    loads = [pltpu.make_async_copy(half(ctr, yh), z_piece(0, 0), lsem.at[0])]
    loads += [
        pltpu.make_async_copy(half(pts, yh, r * hrow, hrow), px.at[UNIT[OWN, r], yh], lsem.at[1 + r])
        for r in range(2)
    ]
    for cp in loads:
        cp.start()

    barrier = pltpu.get_barrier_semaphore()
    near = [dev(z_=zat(r)) for r in (1, -1, 2, -2)] + [d_xp, d_xm, d_x2, d_yp, d_ym, d_y2, d_sib]
    near += [dev(yh_=oh, z_=zat(r)) for r in (1, -1, 2, -2)]
    w_to = [dev(yh_=(y + n) % NY // 2, x_=q, q_=(y + n) % NY % 2 * 2 + cc) for n in range(NY) for cc in (c, 1 - c)]
    for other in near:
        pl.semaphore_signal(barrier, inc=1, device_id=other, device_id_type=MESH)
    for n, other in enumerate(w_to):
        if n:
            pl.semaphore_signal(barrier, inc=1, device_id=other, device_id_type=MESH)
    w_from = [dev(yh_=yh ^ n, x_=(q + m) % NX, q_=x) for n in range(2) for m in range(NX)]
    for n, other in enumerate(w_from):
        if n:
            pl.semaphore_signal(barrier, inc=1, device_id=other, device_id_type=MESH)

    @pl.when(jnp.logical_not(diag))
    def _():
        pl.semaphore_signal(barrier, inc=1, device_id=w_to[0], device_id_type=MESH)
        pl.semaphore_signal(barrier, inc=1, device_id=w_from[0], device_id_type=MESH)
        pl.semaphore_wait(barrier, len(near) + len(w_to) + len(w_from))

    @pl.when(diag)
    def _():
        pl.semaphore_wait(barrier, len(near) + len(w_to) + len(w_from) - 2)

    o_z, o_zw = new_s(), new_s()
    i_step = [{2: new(), 4: new(), 6: new()} for _ in range(3)]
    i_near, i_far, i_wrest = new(), new(), new()
    sign = (1, -1)

    def z_sem(kind, dist):
        if dist in i_step[kind]:
            return i_step[kind][dist]
        return i_wrest if kind == 2 else i_near if dist < 4 else i_far

    def z_there(d, kind, dist):
        return dist < HALF or (kind == 1) == (d == 1)

    def z_hop(d, kind, dist, src=None):
        for hop in (2, 1):
            if dist + hop <= HALF and z_there(d, kind, dist + hop):
                piece = z_piece(kind, -sign[d] * dist) if src is None else src
                send(o_zw if kind == 2 else o_z, z_sem(kind, dist + hop), piece,
                     z_piece(kind, -sign[d] * (dist + hop)), dev(z_=zat(sign[d] * hop)))

    def z_step(kind, dist):
        arrive(i_step[kind][dist], wx.at[0:2] if kind == 2 else cx.at[0])
        for d in range(2):
            z_hop(d, kind, dist)

    for d in range(2):
        z_hop(d, 0, 0, half(ctr, yh))
    o_sc, i_sc = new_s(), new()
    for d in range(2):
        for hop in (2, 1):
            send(o_z, z_sem(1, hop), half(ctr, oh), ctr_at(yh, -sign[d] * hop), dev(yh_=oh, z_=zat(sign[d] * hop)))
    send(o_sc, i_sc, half(ctr, oh), ctr_at(yh, 0), d_y2)

    o_x, o_sp = new_s(), new_s()
    i_sp = [new(), new()]
    i_x = [[new(), new()] for _ in range(2)]
    i_xo = [new(), new()]
    i_xf = new()
    x_to = ((d_xp, LEFT), (d_xm, RIGHT))

    def x_own(d, j, r, src=None):
        yy = oh if j else yh
        to, slot = x_to[d]
        src = px.at[UNIT[OWN, r], yy] if src is None else src
        send(o_x, i_x[d][j] if r == d else i_xo[j], src, px.at[UNIT[slot, r], yy], to)

    def x_pass(d, j):
        yy = oh if j else yh
        piece = px.at[UNIT[(LEFT, RIGHT)[d], d], yy]
        arrive(i_x[d][j], piece)
        send(o_x, i_xf, piece, px.at[UNIT[FAR, d], yy], x_to[d][0])

    for r in range(2):
        x_own(0, 0, r, half(pts, yh, r * hrow, hrow))
        x_own(1, 0, 1 - r, half(pts, yh, (1 - r) * hrow, hrow))
        send(o_sp, i_sp[r], half(pts, oh, r * hrow, hrow), px.at[UNIT[OWN, r], yh], d_y2)

    o_w, o_w0, i_w = new_s(), new_s(), new()

    def w_copy(n, local=False):
        src = wts.at[:, pl.ds(pl.multiple_of((c ^ (n % 2)) * lab, 128), lab)]
        if local:
            return pltpu.make_async_copy(src, wx.at[0, x, yh], rsem.at[i_w])
        return copy(o_w if n else o_w0, i_w, src, wx.at[0, x, yh], w_to[n])

    for n in range(1, 8):
        w_copy(n).start()

    @pl.when(jnp.logical_not(diag))
    def _():
        w_copy(0).start()

    @pl.when(diag)
    def _():
        w_copy(0, True).start()

    def square(v):
        v = v.astype(F32)
        return jnp.sum(v * v, axis=1, keepdims=True)

    csq = [None, None]

    def centers(s):
        return cx[s * HALF : (s + 1) * HALF].reshape(cset, feats)

    def set_ready(s):
        sq = square(centers(s))
        csq[s] = jnp.transpose(jnp.broadcast_to(sq, (sq.shape[0], 128)))[0:1, :]

    srow = hrow // NY
    o_dc, i_dc = new_s(), [new() for _ in range(NP)]

    def tiles(i):
        lo, hi, s = PIECES[i]
        n = (hi - lo) * 2 * hrow
        p = px[lo:hi].reshape(n, feats)
        if s == 0:
            psq[lo * 2 * hrow : hi * 2 * hrow] = square(p)
        cross = lax.dot_general(p, centers(s), (((1,), (1,)), ((), ())), preferred_element_type=F32)
        part = psq[lo * 2 * hrow : hi * 2 * hrow] + csq[s] - 2.0 * cross
        dpart[i][...] = part.reshape(hi - lo, 2, hrow, cset)
        send(o_dc, i_dc[i], dpart[i].at[:, 1 - c], dcore[i], d_sib)

    def scatter(o, total, v1, v2):
        i1, i2 = new(), new()

        def first():
            send(o, i1, total(y2, 0), v1.at[0], d_yp)
            send(o, i1, total(y2, 1), v1.at[1], d_ym)

        def second():
            arrive(i1, v1)
            for h, y_ in enumerate((yp, ym)):
                ref = total(y_, h)
                ref[...] = ref[...] + v1[h]
            send(o, i2, total(yp, None), v2.at[0], d_yp)
            send(o, i2, total(ym, None), v2.at[1], d_ym)

        def third():
            arrive(i2, v2)
            return total(y, None)[...] + v2[0] + v2[1]

        return first, second, third

    def d_slice(i):
        n = PIECES[i][1] - PIECES[i][0]

        def total(t, h):
            units = pl.ds(0, n) if h is None else pl.ds(h * (n // 2), n // 2)
            return dpart[i].at[units, c, pl.ds(pl.multiple_of(t * srow, 16), srow)]

        return total

    o_dr = new_s()
    d_ring = [scatter(o_dr, d_slice(i), r1[i], r2[i]) for i in range(NP)]

    def d_first(i):
        arrive(i_dc[i], dcore[i])
        dpart[i][:, c] = dpart[i][:, c] + dcore[i][...]
        d_ring[i][0]()

    o_k, i_k = new_s(), [new() for _ in range(4)]
    k_to = (d_xp, d_xm, d_x2, d_sib)

    def d_third(i):
        dist = d_ring[i][2]()
        val = jnp.exp(dist * (-inv_f)).astype(BF16)
        lo, hi, s = PIECES[i]
        for j in range(hi - lo):
            k, r = UNITS[lo + j]
            ref = kx.at[x, c, s, pl.ds(pl.multiple_of((xabs[k] * 2 + r) * srow, 16), srow)]
            ref[...] = val[j]
            for n, to in enumerate(k_to):
                send(o_k, i_k[n], ref, ref, to)

    z_step(0, 2)
    z_step(1, 2)
    arrive(i_sp[0], px.at[UNIT[OWN, 0], oh])
    x_own(0, 1, 0)
    x_pass(0, 0)
    x_pass(1, 0)
    z_step(0, 4)
    arrive(i_sp[1], px.at[UNIT[OWN, 1], oh])
    x_own(0, 1, 1)
    x_own(1, 1, 1)
    x_own(1, 1, 0)
    z_step(1, 4)
    for cp in loads:
        cp.wait()
    arrive(i_sc, z_piece(1, 0))
    arrive(i_near, cx.at[0:4])
    set_ready(0)
    tiles(0)
    z_step(0, 6)
    z_step(1, 6)
    arrive(i_w, wx.at[0])
    for d in range(2):
        z_hop(d, 2, 0)
    arrive(i_xo[0], px.at[0])
    x_pass(0, 1)
    x_pass(1, 1)
    d_first(0)
    tiles(1)
    d_first(1)
    d_ring[0][1]()
    arrive(i_xo[1], px.at[0])
    z_step(2, 2)
    d_ring[1][1]()
    arrive(i_xf, px.at[6:8])
    tiles(2)
    arrive(i_far, cx.at[0:5])
    set_ready(1)
    tiles(3)
    d_first(2)
    tiles(4)
    d_first(3)
    d_first(4)
    z_step(2, 4)
    d_third(0)
    d_third(1)
    d_ring[2][1]()
    d_ring[3][1]()
    d_ring[4][1]()
    z_step(2, 6)
    d_third(2)
    d_third(3)
    d_third(4)
    arrive(i_wrest, wx.at[0:9])

    for n, xs in enumerate((xm, xp, x2)):
        arrive(i_k[n], kx.at[xs, c])
        send(o_k, i_k[3], kx.at[xs, c], kx.at[xs, c], d_sib)

    def fit_of(cc):
        fit = None
        for xs in range(NX):
            for s in range(2):
                w = wx[s * HALF : (s + 1) * HALF, xs].reshape(cset, lab)
                term = jnp.dot(kx[xs, cc, s], w, preferred_element_type=F32)
                fit = term if fit is None else fit + term
        return fit.astype(BF16)

    def keep(cc):
        fitted[pl.ds(pl.multiple_of(cc * 2 * hrow, 16), 2 * hrow)] = fit_of(cc)

    keep(c)
    arrive(i_k[3], kx.at[:, 1 - c])
    keep(1 - c)

    for y_ in (y2, yp, ym, y):
        for s in range(2):
            kk = kx[y_, :, s].reshape(4 * hrow, cset)
            gsum[y_, s * cset : (s + 1) * cset] = lax.dot_general(
                kk, fitted[...], (((0,), (0,)), ((), ())), preferred_element_type=F32
            )

    grow = 2 * cset // 4
    zper = NZ // 4
    o_g, o_za, o_zn, o_z1, o_z0 = (new_s() for _ in range(5))
    i_za, i_zn, i_z0 = new(), new(), [new(), new()]
    own = jnp.logical_and(diag, y == x)

    def g_rows(rel, yy=None):
        slot = SLOT[rel]
        if yy is None:
            return gout.at[slot * 2 * crow : (slot + 1) * 2 * crow]
        return gout.at[pl.ds(pl.multiple_of((2 * slot + yy) * crow, 16), crow)]

    def z_final(rel, n):
        yy = yh ^ n
        out_sem = o_zn if rel else (o_z0, o_z1)[n]
        j = NEAR.index(rel)
        to = dev(yh_=yy, x_=y, z_=zat(rel), q_=x)
        src = g_rows(rel, yy)
        if rel:
            return copy(out_sem, i_zn, src, zb.at[c, j], to)
        return pltpu.make_async_remote_copy(
            src_ref=src, dst_ref=zb.at[c, j], send_sem=ssem.at[out_sem], recv_sem=rsem.at[i_z0[0] + c],
            device_id=to, device_id_type=MESH,
        )

    def z0_arrive(cc):
        ref = zb.at[cc, 0]
        pltpu.make_async_remote_copy(
            src_ref=ref, dst_ref=ref, send_sem=ssem.at[o_z0], recv_sem=rsem.at[i_z0[0] + cc],
            device_id=d_sib, device_id_type=MESH,
        ).wait_recv()

    def z_relay(rel):
        if rel == HALF:
            for d in range(2):
                rows = pl.ds(d * crow, crow)
                src = gout.at[pl.ds((2 * SLOT[rel] + d) * crow, crow)]
                send(o_za, i_za, src, za.at[6, rows], dev(z_=zat(4 * sign[d])))
            return
        d = 0 if rel > 0 else 1
        hop = abs(rel) - 4
        send(o_za, i_za, g_rows(rel), za.at[2 * (hop - 1) + d], dev(z_=zat(sign[d] * hop)))

    def g_slice(p):
        def total(t, h):
            lo, num = (0, grow) if h is None else (h * (grow // 2), grow // 2)
            return gsum.at[t, pl.ds(p * grow + lo, num)]

        return total

    order = (3, 2, 1, 0)
    g_ring = [scatter(o_g, g_slice(p), g1.at[p], g2.at[p]) for p in range(4)]
    for stage in range(2):
        for p in order:
            g_ring[p][stage]()
    for p in order:
        gout[p * grow : (p + 1) * grow] = g_ring[p][2]()
        for rel in reversed(REL[p * zper : (p + 1) * zper]):
            if abs(rel) > 4:
                z_relay(rel)
            elif rel and abs(rel) < 4:
                for n in range(2):
                    z_final(rel, n).start()
    z_final(0, 1).start()

    @pl.when(own)
    def _():
        zb[c, 0] = g_rows(0, yh)[...]

    arrive(i_za, za)
    for d, rel in enumerate((4, -4)):
        ref = g_rows(rel)
        ref[...] = ref[...] + za[d] + za[2 + d] + za[4 + d]
        part = gout.at[pl.ds((2 * SLOT[rel] + d) * crow, crow)]
        part[...] = part[...] + za[6, d * crow : (d + 1) * crow]
        for n in range(2):
            z_final(rel, n).start()

    @pl.when(jnp.logical_not(own))
    def _():
        z_final(0, 0).start()
        z0_arrive(c)

    z0_arrive(1 - c)
    arrive(i_zn, zb.at[:, 1:])
    for cc in range(2):
        total = zb[cc, 0]
        for j in range(1, len(NEAR)):
            total = total + zb[cc, j]
        out[:, cc * lab : (cc + 1) * lab] = total * scale

    sent(o_z, cx.at[0 : NZ - 1])
    sent(o_zw, wx.at[0 : NZ - 1])
    sent(o_sc, cx.at[0, 0])
    sent(o_x, px.at[0:6])
    sent(o_sp, px.at[0])
    sent(o_w, wx.at[0:7, 0, 0])
    sent(o_dc, cx)
    sent(o_dr, px.at[0:3])
    sent(o_k, cx.at[0:14])
    sent(o_g, px.at[0:3])
    sent(o_za, za)
    sent(o_zn, zb.at[:, 1:])
    sent(o_z1, zb.at[0, 0])

    @pl.when(jnp.logical_not(diag))
    def _():
        sent(o_w0, wx.at[0, 0, 0])

    @pl.when(jnp.logical_not(own))
    def _():
        sent(o_z0, zb.at[0, 0])


def solution(mesh):
    assert mesh.shape["blk"] == 2 * NX * NZ and mesh.shape["feat"] == 4

    def step(points, centers, coefs):
        rows, qf = points.shape
        crow, labels = coefs.shape
        feats, cset, lab = qf // 2, 2 * HALF * crow, labels // 2
        npts = rows * mesh.shape["blk"]
        nf = qf * mesh.shape["feat"]
        srow, grow, cols = rows // 2 // NY, 2 * cset // 4, cset
        V = pltpu.VMEM
        per_piece = [
            [V(shape(hi - lo), F32) for lo, hi, _ in PIECES]
            for shape in (
                lambda n: (n, 2, rows // 2, cols),
                lambda n: (n, rows // 2, cols),
                lambda n: (2, n // 2, srow, cols),
                lambda n: (2, n, srow, cols),
            )
        ]
        return pl.pallas_call(
            functools.partial(kernel, 1.0 / nf, 1.0 / math.sqrt(npts)),
            out_shape=jax.ShapeDtypeStruct((crow, labels), F32),
            in_specs=[pl.BlockSpec(memory_space=pl.ANY)] * 3,
            out_specs=pl.BlockSpec(memory_space=pltpu.VMEM),
            scratch_shapes=[
                V((2 * NX, 2, rows // 2, feats), BF16),
                V((NZ, 2, crow, feats), BF16),
                V((NZ, NX, 2, crow, lab), BF16),
                V((NX, 2, 2, rows, cset), BF16),
                V((4, 2 * cset, lab), F32),
                V((2 * cset, lab), F32),
                V((2, len(NEAR), crow, lab), F32),
                V((4, 2, grow // 2, lab), F32),
                V((4, 2, grow, lab), F32),
                V((7, 2 * crow, lab), F32),
                V((8 * rows, 1), F32),
                V((2 * rows, lab), BF16),
                *[v for group in per_piece for v in group],
                pltpu.SemaphoreType.DMA((SENDS,)),
                pltpu.SemaphoreType.DMA((ARRIVALS,)),
                pltpu.SemaphoreType.DMA((3,)),
            ],
            compiler_params=pltpu.CompilerParams(collective_id=0, has_side_effects=True),
        )(points, centers, coefs)

    spec = P("blk", "feat")
    return jax.shard_map(
        step, mesh=mesh, in_specs=(spec, spec, spec), out_specs=spec, check_vma=False
    )
```

```python
import functools
import math

import jax
import jax.numpy as jnp
from jax import lax
from jax.experimental import pallas as pl
from jax.experimental.pallas import tpu as pltpu
from jax.sharding import PartitionSpec as P

MESH = pl.DeviceIdType.MESH
F32, BF16 = jnp.float32, jnp.bfloat16
NX, NY, NZ = 4, 4, 16
SENDS, ARRIVALS = 15, 60
REL = [0] + [s * d for d in range(1, NZ // 2) for s in (1, -1)] + [NZ // 2]
REL.remove(4), REL.insert(7, 4)
SLOT = {r: i for i, r in enumerate(REL)}
HALF = NZ // 2
OWN, LEFT, RIGHT, FAR = range(4)
UNITS = ((OWN, 0), (OWN, 1), (LEFT, 0), (RIGHT, 1), (LEFT, 1), (RIGHT, 0), (FAR, 0), (FAR, 1))
UNIT = {u: i for i, u in enumerate(UNITS)}
PIECES = ((0, 2, 0), (2, 4, 0), (4, 8, 0), (0, 4, 1), (4, 8, 1))
NEAR = [0, 1, -1, 2, -2, 3, -3, 4, -4]
NP = len(PIECES)


def kernel(
    inv_f, scale, pts, ctr, wts, out,
    px, cx, wx, kx, gsum, gout, zb, *rest,
):
    g1, g2, za, psq, fitted = rest[:5]
    dpart, dcore, r1, r2 = (rest[5 + NP * i : 5 + NP * (i + 1)] for i in range(4))
    ssem, rsem, lsem, hello = rest[5 + 4 * NP :]
    b, q = lax.axis_index("blk"), lax.axis_index("feat")
    yh, x, z = b // (NX * NZ), (b // NZ) % NX, b % NZ
    yl, c = q // 2, q % 2
    y, oh = 2 * yh + yl, 1 - yh
    feats = pts.shape[1] // 2
    hrow = pts.shape[0] // 2
    crow = ctr.shape[0]
    cset = 2 * HALF * crow
    lab = wts.shape[1] // 2

    def dev(yh_=None, x_=None, z_=None, q_=None):
        yh_ = yh if yh_ is None else yh_
        x_ = x if x_ is None else x_
        z_ = z if z_ is None else z_
        return ((yh_ * NX + x_) * NZ + z_, q if q_ is None else q_)

    def ydev(y_):
        return dev(yh_=y_ // 2, q_=(y_ % 2) * 2 + c)

    def zat(rel):
        return (z + rel + NZ) % NZ

    xp, xm, x2 = (x + 1) % NX, (x + 3) % NX, (x + 2) % NX
    xabs = (x, xm, xp, x2)
    yp, ym, y2 = (y + 1) % NY, (y + 3) % NY, (y + 2) % NY
    d_xp, d_xm, d_x2 = dev(x_=xp), dev(x_=xm), dev(x_=x2)
    d_yp, d_ym, d_y2 = ydev(yp), ydev(ym), ydev(y2)
    d_sib = dev(q_=2 * yl + 1 - c)
    diag = x == q

    used = [0, 0]

    def counter(which, limit):
        def new():
            used[which] += 1
            assert used[which] <= limit
            return used[which] - 1
        return new

    new_s, new = counter(0, SENDS), counter(1, ARRIVALS)

    def copy(o, i, src, dst, to):
        return pltpu.make_async_remote_copy(
            src_ref=src, dst_ref=dst, send_sem=ssem.at[o], recv_sem=rsem.at[i],
            device_id=to, device_id_type=MESH,
        )

    def send(o, i, src, dst, to):
        copy(o, i, src, dst, to).start()

    def arrive(i, ref):
        copy(0, i, ref, ref, d_sib).wait_recv()

    def sent(o, ref):
        copy(o, 0, ref, ref, d_sib).wait_send()

    def half(ref, h, lo=0, num=None):
        num = ref.shape[0] if num is None else num
        return ref.at[pl.ds(lo, num), pl.ds(pl.multiple_of(h * feats, 128), feats)]

    def ctr_at(yh_, rel):
        return cx.at[SLOT[HALF if rel == -HALF else rel], yh_]

    def z_piece(kind, rel):
        if kind == 2:
            return wx.at[SLOT[HALF if rel == -HALF else rel]]
        return ctr_at(oh if kind == 1 else yh, rel)

    loads = [pltpu.make_async_copy(half(ctr, yh), z_piece(0, 0), lsem.at[0])]
    loads += [
        pltpu.make_async_copy(half(pts, yh, r * hrow, hrow), px.at[UNIT[OWN, r], yh], lsem.at[1 + r])
        for r in range(2)
    ]
    for cp in loads:
        cp.start()

    barrier = pltpu.get_barrier_semaphore()
    near = [dev(z_=zat(r)) for r in (1, -1, 2, -2)] + [d_xp, d_xm, d_x2, d_yp, d_ym, d_y2, d_sib]
    w_to = [dev(yh_=(y + n) % NY // 2, x_=q, q_=(y + n) % NY % 2 * 2 + cc) for n in range(NY) for cc in (c, 1 - c)]

    def greet(sem, others):
        for other in others:
            pl.semaphore_signal(sem, inc=1, device_id=other, device_id_type=MESH)

    greet(barrier, near)
    pl.semaphore_wait(barrier, len(near))
    greet(hello.at[0], [d_y2])
    greet(hello.at[1], near)

    o_z, o_zw = new_s(), new_s()
    PARTS = 2
    i_step = [{n: [new() for _ in range(PARTS if kind < 2 else 1)] for n in (2, 4, 6)} for kind in range(3)]
    i_near, i_far, i_wrest = new(), new(), new()
    sign = (1, -1)

    def z_there(d, kind, dist):
        return dist < HALF or (kind == 1) == (d == 1)

    def z_part(ref, part):
        return ref.at[:, part * (feats // PARTS) : (part + 1) * (feats // PARTS)]

    def z_two(d, kind, dist, part, src=None, dst=None, to=None):
        if not z_there(d, kind, dist + 2):
            return
        src = z_piece(kind, -sign[d] * dist) if src is None else src
        dst = z_piece(kind, -sign[d] * (dist + 2)) if dst is None else dst
        to = dev(z_=zat(2 * sign[d])) if to is None else to
        i = i_step[kind][dist + 2][part] if dist + 2 in i_step[kind] else i_wrest if kind == 2 else i_far
        if kind == 2:
            return send(o_zw, i, src, dst, to)
        send(o_z, i, z_part(src, part), z_part(dst, part), to)

    def z_one(d, kind, dist, src=None, dst=None, to=None):
        src = z_piece(kind, -sign[d] * dist) if src is None else src
        dst = z_piece(kind, -sign[d] * (dist + 1)) if dst is None else dst
        to = dev(z_=zat(sign[d])) if to is None else to
        i = i_wrest if kind == 2 else i_near if dist < 4 else i_far
        send(o_zw if kind == 2 else o_z, i, src, dst, to)

    def z_hop(kind, dist):
        for part in range(len(i_step[kind][2])):
            if dist:
                arrive(i_step[kind][dist][part], wx.at[0:2] if kind == 2 else cx.at[0, 0])
            for d in range(2):
                z_two(d, kind, dist, part)
        for d in range(2):
            z_one(d, kind, dist)

    def z_step(kind, dist):
        z_hop(kind, dist)

    mine = half(ctr, yh)
    for part in range(PARTS):
        for d in range(2):
            z_two(d, 0, 0, part, mine)
    for d in range(2):
        z_one(d, 0, 0, mine)
    o_sc, i_sc = new_s(), new()
    send(o_sc, i_sc, half(ctr, oh), ctr_at(yh, 0), d_y2)

    o_x, o_sp = new_s(), new_s()
    i_sp = [new(), new()]
    i_x = [[new(), new()] for _ in range(2)]
    i_xo = [new(), new()]
    i_xf = new()
    x_to = ((d_xp, LEFT), (d_xm, RIGHT))

    def x_own(d, j, r, src=None):
        yy = oh if j else yh
        to, slot = x_to[d]
        src = px.at[UNIT[OWN, r], yy] if src is None else src
        send(o_x, i_x[d][j] if r == d else i_xo[j], src, px.at[UNIT[slot, r], yy], to)

    def x_pass(d, j):
        yy = oh if j else yh
        piece = px.at[UNIT[(LEFT, RIGHT)[d], d], yy]
        arrive(i_x[d][j], piece)
        send(o_x, i_xf, piece, px.at[UNIT[FAR, d], yy], x_to[d][0])

    for r in range(2):
        x_own(0, 0, r, half(pts, yh, r * hrow, hrow))
        x_own(1, 0, 1 - r, half(pts, yh, (1 - r) * hrow, hrow))
        send(o_sp, i_sp[r], half(pts, oh, r * hrow, hrow), px.at[UNIT[OWN, r], yh], d_y2)

    o_w, o_w0, i_w = new_s(), new_s(), new()

    def w_copy(n, local=False):
        src = wts.at[:, pl.ds(pl.multiple_of((c ^ (n % 2)) * lab, 128), lab)]
        if local:
            return pltpu.make_async_copy(src, wx.at[0, x, yh], rsem.at[i_w])
        return copy(o_w if n else o_w0, i_w, src, wx.at[0, x, yh], w_to[n])

    def w_start():
        for n in range(1, 8):
            w_copy(n).start()

        @pl.when(jnp.logical_not(diag))
        def _():
            w_copy(0).start()

        @pl.when(diag)
        def _():
            w_copy(0, True).start()

    pl.semaphore_wait(hello.at[0], 1)
    other = half(ctr, oh)
    for part in range(PARTS):
        for d in range(2):
            z_two(d, 1, 0, part, other, ctr_at(yh, -2 * sign[d]), dev(yh_=oh, z_=zat(2 * sign[d])))
    for d in range(2):
        z_one(d, 1, 0, other, ctr_at(yh, -sign[d]), dev(yh_=oh, z_=zat(sign[d])))

    def square(v):
        v = v.astype(F32)
        return jnp.sum(v * v, axis=1, keepdims=True)

    csq = [None, None]

    def centers(s):
        return cx[s * HALF : (s + 1) * HALF].reshape(cset, feats)

    def set_ready(s):
        sq = square(centers(s))
        csq[s] = jnp.transpose(jnp.broadcast_to(sq, (sq.shape[0], 128)))[0:1, :]

    srow = hrow // NY
    o_dc, i_dc = new_s(), [new() for _ in range(NP)]

    def tiles(i):
        lo, hi, s = PIECES[i]
        n = (hi - lo) * 2 * hrow
        p = px[lo:hi].reshape(n, feats)
        if s == 0:
            psq[lo * 2 * hrow : hi * 2 * hrow] = square(p)
        cross = lax.dot_general(p, centers(s), (((1,), (1,)), ((), ())), preferred_element_type=F32)
        part = psq[lo * 2 * hrow : hi * 2 * hrow] + csq[s] - 2.0 * cross
        dpart[i][...] = part.reshape(hi - lo, 2, hrow, cset)
        send(o_dc, i_dc[i], dpart[i].at[:, 1 - c], dcore[i], d_sib)

    def scatter(o, total, v1, v2):
        i1, i2 = new(), new()

        def first():
            send(o, i1, total(y2, 0), v1.at[0], d_yp)
            send(o, i1, total(y2, 1), v1.at[1], d_ym)

        def second():
            arrive(i1, v1)
            for h, y_ in enumerate((yp, ym)):
                ref = total(y_, h)
                ref[...] = ref[...] + v1[h]
            send(o, i2, total(yp, None), v2.at[0], d_yp)
            send(o, i2, total(ym, None), v2.at[1], d_ym)

        def third():
            arrive(i2, v2)
            return total(y, None)[...] + v2[0] + v2[1]

        return first, second, third

    def d_slice(i):
        n = PIECES[i][1] - PIECES[i][0]

        def total(t, h):
            units = pl.ds(0, n) if h is None else pl.ds(h * (n // 2), n // 2)
            return dpart[i].at[units, c, pl.ds(pl.multiple_of(t * srow, 16), srow)]

        return total

    o_dr = new_s()
    d_ring = [scatter(o_dr, d_slice(i), r1[i], r2[i]) for i in range(NP)]

    def d_first(i):
        arrive(i_dc[i], dcore[i])
        dpart[i][:, c] = dpart[i][:, c] + dcore[i][...]
        d_ring[i][0]()

    o_k, i_k = new_s(), [new() for _ in range(4)]
    k_to = (d_xp, d_xm, d_x2, d_sib)

    def d_third(i):
        dist = d_ring[i][2]()
        val = jnp.exp(dist * (-inv_f)).astype(BF16)
        lo, hi, s = PIECES[i]
        for j in range(hi - lo):
            k, r = UNITS[lo + j]
            ref = kx.at[x, c, s, pl.ds(pl.multiple_of((xabs[k] * 2 + r) * srow, 16), srow)]
            ref[...] = val[j]
            for n, to in enumerate(k_to):
                send(o_k, i_k[n], ref, ref, to)

    z_step(0, 2)
    pl.semaphore_wait(hello.at[1], len(near))
    greet(hello.at[2], near)
    x_pass(0, 0)
    x_pass(1, 0)
    z_step(1, 2)
    arrive(i_sp[0], px.at[UNIT[OWN, 0], oh])
    x_own(0, 1, 0)
    z_step(0, 4)
    pl.semaphore_wait(hello.at[2], len(near))
    w_start()
    arrive(i_sp[1], px.at[UNIT[OWN, 1], oh])
    x_own(0, 1, 1)
    x_own(1, 1, 1)
    x_own(1, 1, 0)
    z_step(1, 4)
    for cp in loads:
        cp.wait()
    arrive(i_sc, z_piece(1, 0))
    arrive(i_near, cx.at[0:4])
    set_ready(0)
    tiles(0)
    z_step(0, 6)
    x_pass(0, 1)
    x_pass(1, 1)
    z_step(1, 6)
    arrive(i_xo[0], px.at[0])
    d_first(0)
    tiles(1)
    arrive(i_w, wx.at[0])
    z_hop(2, 0)
    d_first(1)
    arrive(i_far, cx.at[0:5])
    set_ready(1)
    tiles(3)
    d_ring[0][1]()
    z_step(2, 2)
    d_first(3)
    arrive(i_xo[1], px.at[0])
    arrive(i_xf, px.at[6:8])
    tiles(2)
    tiles(4)
    d_ring[1][1]()
    d_first(2)
    d_ring[3][1]()
    d_first(4)
    z_step(2, 4)
    d_third(0)
    d_third(1)
    d_ring[2][1]()
    d_ring[4][1]()
    d_third(3)
    z_step(2, 6)
    d_third(2)
    d_third(4)
    arrive(i_wrest, wx.at[0:9])

    for n, xs in enumerate((xm, xp, x2)):
        arrive(i_k[n], kx.at[xs, c])
        send(o_k, i_k[3], kx.at[xs, c], kx.at[xs, c], d_sib)

    def fit_of(cc):
        fit = None
        for xs in range(NX):
            for s in range(2):
                w = wx[s * HALF : (s + 1) * HALF, xs].reshape(cset, lab)
                term = jnp.dot(kx[xs, cc, s], w, preferred_element_type=F32)
                fit = term if fit is None else fit + term
        return fit.astype(BF16)

    def keep(cc):
        fitted[pl.ds(pl.multiple_of(cc * 2 * hrow, 16), 2 * hrow)] = fit_of(cc)

    keep(c)
    arrive(i_k[3], kx.at[:, 1 - c])
    keep(1 - c)

    for y_ in (y2, yp, ym, y):
        for s in range(2):
            kk = kx[y_, :, s].reshape(4 * hrow, cset)
            gsum[y_, s * cset : (s + 1) * cset] = lax.dot_general(
                kk, fitted[...], (((0,), (0,)), ((), ())), preferred_element_type=F32
            )

    grow = 2 * cset // 4
    zper = NZ // 4
    o_g, o_za, o_zn, o_z1, o_z0 = (new_s() for _ in range(5))
    i_za, i_zn, i_z0 = new(), new(), [new(), new()]
    own = jnp.logical_and(diag, y == x)

    def g_rows(rel, yy=None):
        slot = SLOT[rel]
        if yy is None:
            return gout.at[slot * 2 * crow : (slot + 1) * 2 * crow]
        return gout.at[pl.ds(pl.multiple_of((2 * slot + yy) * crow, 16), crow)]

    def z_final(rel, n):
        yy = yh ^ n
        out_sem = o_zn if rel else (o_z0, o_z1)[n]
        j = NEAR.index(rel)
        to = dev(yh_=yy, x_=y, z_=zat(rel), q_=x)
        src = g_rows(rel, yy)
        if rel:
            return copy(out_sem, i_zn, src, zb.at[c, j], to)
        return pltpu.make_async_remote_copy(
            src_ref=src, dst_ref=zb.at[c, j], send_sem=ssem.at[out_sem], recv_sem=rsem.at[i_z0[0] + c],
            device_id=to, device_id_type=MESH,
        )

    def z0_arrive(cc):
        ref = zb.at[cc, 0]
        pltpu.make_async_remote_copy(
            src_ref=ref, dst_ref=ref, send_sem=ssem.at[o_z0], recv_sem=rsem.at[i_z0[0] + cc],
            device_id=d_sib, device_id_type=MESH,
        ).wait_recv()

    def z_relay(rel):
        if rel == HALF:
            for d in range(2):
                rows = pl.ds(d * crow, crow)
                src = gout.at[pl.ds((2 * SLOT[rel] + d) * crow, crow)]
                send(o_za, i_za, src, za.at[6, rows], dev(z_=zat(4 * sign[d])))
            return
        d = 0 if rel > 0 else 1
        hop = abs(rel) - 4
        send(o_za, i_za, g_rows(rel), za.at[2 * (hop - 1) + d], dev(z_=zat(sign[d] * hop)))

    def g_slice(p):
        def total(t, h):
            lo, num = (0, grow) if h is None else (h * (grow // 2), grow // 2)
            return gsum.at[t, pl.ds(p * grow + lo, num)]

        return total

    order = (3, 2, 1, 0)
    g_ring = [scatter(o_g, g_slice(p), g1.at[p], g2.at[p]) for p in range(4)]
    for stage in range(2):
        for p in order:
            g_ring[p][stage]()
    for p in order:
        gout[p * grow : (p + 1) * grow] = g_ring[p][2]()
        for rel in reversed(REL[p * zper : (p + 1) * zper]):
            if abs(rel) > 4:
                z_relay(rel)
            elif rel and abs(rel) < 4:
                for n in range(2):
                    z_final(rel, n).start()
    z_final(0, 1).start()

    @pl.when(own)
    def _():
        zb[c, 0] = g_rows(0, yh)[...]

    arrive(i_za, za)
    for d, rel in enumerate((4, -4)):
        ref = g_rows(rel)
        ref[...] = ref[...] + za[d] + za[2 + d] + za[4 + d]
        part = gout.at[pl.ds((2 * SLOT[rel] + d) * crow, crow)]
        part[...] = part[...] + za[6, d * crow : (d + 1) * crow]
        for n in range(2):
            z_final(rel, n).start()

    @pl.when(jnp.logical_not(own))
    def _():
        z_final(0, 0).start()
        z0_arrive(c)

    z0_arrive(1 - c)
    arrive(i_zn, zb.at[:, 1:])
    for cc in range(2):
        total = zb[cc, 0]
        for j in range(1, len(NEAR)):
            total = total + zb[cc, j]
        out[:, cc * lab : (cc + 1) * lab] = total * scale

    assert used == [SENDS, ARRIVALS], used
    sent(o_z, cx.at[0 : NZ - 1])
    sent(o_zw, wx.at[0 : NZ - 1])
    sent(o_sc, cx.at[0, 0])
    sent(o_x, px.at[0:6])
    sent(o_sp, px.at[0])
    sent(o_w, wx.at[0:7, 0, 0])
    sent(o_dc, cx)
    sent(o_dr, px.at[0:3])
    sent(o_k, cx.at[0:14])
    sent(o_g, px.at[0:3])
    sent(o_za, za)
    sent(o_zn, zb.at[:, 1:])
    sent(o_z1, zb.at[0, 0])

    @pl.when(jnp.logical_not(diag))
    def _():
        sent(o_w0, wx.at[0, 0, 0])

    @pl.when(jnp.logical_not(own))
    def _():
        sent(o_z0, zb.at[0, 0])


def solution(mesh):
    assert mesh.shape["blk"] == 2 * NX * NZ and mesh.shape["feat"] == 4

    def step(points, centers, coefs):
        rows, qf = points.shape
        crow, labels = coefs.shape
        feats, cset, lab = qf // 2, 2 * HALF * crow, labels // 2
        npts = rows * mesh.shape["blk"]
        nf = qf * mesh.shape["feat"]
        srow, grow, cols = rows // 2 // NY, 2 * cset // 4, cset
        V = pltpu.VMEM
        per_piece = [
            [V(shape(hi - lo), F32) for lo, hi, _ in PIECES]
            for shape in (
                lambda n: (n, 2, rows // 2, cols),
                lambda n: (n, rows // 2, cols),
                lambda n: (2, n // 2, srow, cols),
                lambda n: (2, n, srow, cols),
            )
        ]
        return pl.pallas_call(
            functools.partial(kernel, 1.0 / nf, 1.0 / math.sqrt(npts)),
            out_shape=jax.ShapeDtypeStruct((crow, labels), F32),
            in_specs=[pl.BlockSpec(memory_space=pl.ANY)] * 3,
            out_specs=pl.BlockSpec(memory_space=pltpu.VMEM),
            scratch_shapes=[
                V((2 * NX, 2, rows // 2, feats), BF16),
                V((NZ, 2, crow, feats), BF16),
                V((NZ, NX, 2, crow, lab), BF16),
                V((NX, 2, 2, rows, cset), BF16),
                V((4, 2 * cset, lab), F32),
                V((2 * cset, lab), F32),
                V((2, len(NEAR), crow, lab), F32),
                V((4, 2, grow // 2, lab), F32),
                V((4, 2, grow, lab), F32),
                V((7, 2 * crow, lab), F32),
                V((8 * rows, 1), F32),
                V((2 * rows, lab), BF16),
                *[v for group in per_piece for v in group],
                pltpu.SemaphoreType.DMA((SENDS,)),
                pltpu.SemaphoreType.DMA((ARRIVALS,)),
                pltpu.SemaphoreType.DMA((3,)),
                pltpu.SemaphoreType.REGULAR((3,)),
            ],
            compiler_params=pltpu.CompilerParams(collective_id=0, has_side_effects=True),
        )(points, centers, coefs)

    spec = P("blk", "feat")
    return jax.shard_map(
        step, mesh=mesh, in_specs=(spec, spec, spec), out_specs=spec, check_vma=False
    )
```

```python
import functools
import math

import jax
import jax.numpy as jnp
from jax import lax
from jax.experimental import pallas as pl
from jax.experimental.pallas import tpu as pltpu
from jax.sharding import PartitionSpec as P

MESH = pl.DeviceIdType.MESH
F32, BF16 = jnp.float32, jnp.bfloat16
NX, NY, NZ = 4, 4, 16
SENDS, ARRIVALS = 15, 60
REL = [0] + [s * d for d in range(1, NZ // 2) for s in (1, -1)] + [NZ // 2]
REL.remove(4), REL.insert(7, 4)
SLOT = {r: i for i, r in enumerate(REL)}
HALF = NZ // 2
OWN, LEFT, RIGHT, FAR = range(4)
UNITS = ((OWN, 0), (OWN, 1), (LEFT, 0), (RIGHT, 1), (LEFT, 1), (RIGHT, 0), (FAR, 0), (FAR, 1))
UNIT = {u: i for i, u in enumerate(UNITS)}
PIECES = ((0, 2, 0), (2, 4, 0), (4, 8, 0), (0, 4, 1), (4, 8, 1))
NEAR = [0, 1, -1, 2, -2, 3, -3, 4, -4]
NP = len(PIECES)
STOPS = ((0, 2, 4, 6, 8),) * 3


def kernel(
    inv_f, scale, pts, ctr, wts, out,
    px, cx, wx, kx, gsum, gout, zb, *rest,
):
    g1, g2, za, psq, fitted = rest[:5]
    dpart, dcore, r1, r2 = (rest[5 + NP * i : 5 + NP * (i + 1)] for i in range(4))
    ssem, rsem, lsem, hello = rest[5 + 4 * NP :]
    b, q = lax.axis_index("blk"), lax.axis_index("feat")
    yh, x, z = b // (NX * NZ), (b // NZ) % NX, b % NZ
    yl, c = q // 2, q % 2
    y, oh = 2 * yh + yl, 1 - yh
    feats = pts.shape[1] // 2
    hrow = pts.shape[0] // 2
    crow = ctr.shape[0]
    cset = 2 * HALF * crow
    lab = wts.shape[1] // 2

    def dev(yh_=None, x_=None, z_=None, q_=None):
        yh_ = yh if yh_ is None else yh_
        x_ = x if x_ is None else x_
        z_ = z if z_ is None else z_
        return ((yh_ * NX + x_) * NZ + z_, q if q_ is None else q_)

    def ydev(y_):
        return dev(yh_=y_ // 2, q_=(y_ % 2) * 2 + c)

    def zat(rel):
        return (z + rel + NZ) % NZ

    xp, xm, x2 = (x + 1) % NX, (x + 3) % NX, (x + 2) % NX
    xabs = (x, xm, xp, x2)
    yp, ym, y2 = (y + 1) % NY, (y + 3) % NY, (y + 2) % NY
    d_xp, d_xm, d_x2 = dev(x_=xp), dev(x_=xm), dev(x_=x2)
    d_yp, d_ym, d_y2 = ydev(yp), ydev(ym), ydev(y2)
    d_sib = dev(q_=2 * yl + 1 - c)
    diag = x == q

    used = [0, 0]

    def counter(which, limit):
        def new():
            used[which] += 1
            assert used[which] <= limit
            return used[which] - 1
        return new

    new_s, new = counter(0, SENDS), counter(1, ARRIVALS)

    def copy(o, i, src, dst, to):
        return pltpu.make_async_remote_copy(
            src_ref=src, dst_ref=dst, send_sem=ssem.at[o], recv_sem=rsem.at[i],
            device_id=to, device_id_type=MESH,
        )

    def send(o, i, src, dst, to):
        copy(o, i, src, dst, to).start()

    def arrive(i, ref):
        copy(0, i, ref, ref, d_sib).wait_recv()

    def sent(o, ref):
        copy(o, 0, ref, ref, d_sib).wait_send()

    def half(ref, h, lo=0, num=None):
        num = ref.shape[0] if num is None else num
        return ref.at[pl.ds(lo, num), pl.ds(pl.multiple_of(h * feats, 128), feats)]

    def ctr_at(yh_, rel):
        return cx.at[SLOT[HALF if rel == -HALF else rel], yh_]

    def z_piece(kind, rel):
        if kind == 2:
            return wx.at[SLOT[HALF if rel == -HALF else rel]]
        return ctr_at(oh if kind == 1 else yh, rel)

    loads = [pltpu.make_async_copy(half(ctr, yh), z_piece(0, 0), lsem.at[0])]
    loads += [
        pltpu.make_async_copy(half(pts, yh, r * hrow, hrow), px.at[UNIT[OWN, r], yh], lsem.at[1 + r])
        for r in range(2)
    ]
    for cp in loads:
        cp.start()

    barrier = pltpu.get_barrier_semaphore()
    near = [dev(z_=zat(r)) for r in (1, -1, 2, -2)] + [d_xp, d_xm, d_x2, d_yp, d_ym, d_y2, d_sib]
    w_to = [dev(yh_=(y + n) % NY // 2, x_=q, q_=(y + n) % NY % 2 * 2 + cc) for n in range(NY) for cc in (c, 1 - c)]

    def greet(sem, others):
        for other in others:
            pl.semaphore_signal(sem, inc=1, device_id=other, device_id_type=MESH)

    greet(barrier, near)
    pl.semaphore_wait(barrier, len(near))
    greet(hello.at[0], near)

    o_z, o_zw = new_s(), new_s()
    PARTS = 2
    PARTS = 2
    i_step = [{n: [new() for _ in range(PARTS if kind < 2 else 1)] for n in STOPS[kind][1:-1]} for kind in range(3)]
    i_near, i_far, i_wrest = new(), new(), new()
    sign = (1, -1)

    def z_there(d, kind, dist):
        return dist < HALF or (kind == 1) == (d == 1)

    def z_part(ref, part):
        return ref.at[:, part * (feats // PARTS) : (part + 1) * (feats // PARTS)]

    def z_send(d, kind, dist, hop, part=None, src=None):
        if not z_there(d, kind, dist + hop):
            return
        src = z_piece(kind, -sign[d] * dist) if src is None else src
        dst = z_piece(kind, -sign[d] * (dist + hop))
        if dist + hop in i_step[kind]:
            i = i_step[kind][dist + hop][part or 0]
        elif kind == 2:
            i = i_wrest
        else:
            i = i_near if dist + hop < 4 else i_far
        if part is not None:
            src, dst = z_part(src, part), z_part(dst, part)
        send(o_zw if kind == 2 else o_z, i, src, dst, dev(z_=zat(hop * sign[d])))

    def z_step(kind, dist, src=None):
        last = STOPS[kind][STOPS[kind].index(dist) + 1] - dist
        for part in range(PARTS if kind < 2 else 1):
            if dist:
                arrive(i_step[kind][dist][part], wx.at[0:2] if kind == 2 else cx.at[0, 0])
            for d in range(2):
                z_send(d, kind, dist, last, part if kind < 2 else None, src)
        for hop in range(last - 1, 0, -1):
            for d in range(2):
                z_send(d, kind, dist, hop, src=src)

    o_sc, i_sc = new_s(), new()
    send(o_sc, i_sc, half(ctr, oh), ctr_at(yh, 0), d_y2)
    z_step(0, 0, half(ctr, yh))

    o_x, o_sp = new_s(), new_s()
    i_sp = [new(), new()]
    i_x = [[new(), new()] for _ in range(2)]
    i_xo = [new(), new()]
    i_xf = new()
    x_to = ((d_xp, LEFT), (d_xm, RIGHT))

    def x_own(d, j, r, src=None):
        yy = oh if j else yh
        to, slot = x_to[d]
        src = px.at[UNIT[OWN, r], yy] if src is None else src
        send(o_x, i_x[d][j] if r == d else i_xo[j], src, px.at[UNIT[slot, r], yy], to)

    def x_pass(d, j):
        yy = oh if j else yh
        piece = px.at[UNIT[(LEFT, RIGHT)[d], d], yy]
        arrive(i_x[d][j], piece)
        send(o_x, i_xf, piece, px.at[UNIT[FAR, d], yy], x_to[d][0])

    for r in range(2):
        x_own(0, 0, r, half(pts, yh, r * hrow, hrow))
        x_own(1, 0, 1 - r, half(pts, yh, (1 - r) * hrow, hrow))
        send(o_sp, i_sp[r], half(pts, oh, r * hrow, hrow), px.at[UNIT[OWN, r], yh], d_y2)

    o_w, o_w0, i_w = new_s(), new_s(), new()

    def w_copy(n, local=False):
        src = wts.at[:, pl.ds(pl.multiple_of((c ^ (n % 2)) * lab, 128), lab)]
        if local:
            return pltpu.make_async_copy(src, wx.at[0, x, yh], rsem.at[i_w])
        return copy(o_w if n else o_w0, i_w, src, wx.at[0, x, yh], w_to[n])

    def w_start():
        for n in range(1, 8):
            w_copy(n).start()

        @pl.when(jnp.logical_not(diag))
        def _():
            w_copy(0).start()

        @pl.when(diag)
        def _():
            w_copy(0, True).start()

    def square(v):
        v = v.astype(F32)
        return jnp.sum(v * v, axis=1, keepdims=True)

    csq = [None, None]

    def centers(s):
        return cx[s * HALF : (s + 1) * HALF].reshape(cset, feats)

    def set_ready(s):
        sq = square(centers(s))
        csq[s] = jnp.transpose(jnp.broadcast_to(sq, (sq.shape[0], 128)))[0:1, :]

    srow = hrow // NY
    o_dc, i_dc = new_s(), [new() for _ in range(NP)]

    def tiles(i):
        lo, hi, s = PIECES[i]
        n = (hi - lo) * 2 * hrow
        p = px[lo:hi].reshape(n, feats)
        if s == 0:
            psq[lo * 2 * hrow : hi * 2 * hrow] = square(p)
        cross = lax.dot_general(p, centers(s), (((1,), (1,)), ((), ())), preferred_element_type=F32)
        part = psq[lo * 2 * hrow : hi * 2 * hrow] + csq[s] - 2.0 * cross
        dpart[i][...] = part.reshape(hi - lo, 2, hrow, cset)
        send(o_dc, i_dc[i], dpart[i].at[:, 1 - c], dcore[i], d_sib)

    def scatter(o, total, v1, v2):
        i1, i2 = new(), new()

        def first():
            send(o, i1, total(y2, 0), v1.at[0], d_yp)
            send(o, i1, total(y2, 1), v1.at[1], d_ym)

        def second():
            arrive(i1, v1)
            for h, y_ in enumerate((yp, ym)):
                ref = total(y_, h)
                ref[...] = ref[...] + v1[h]
            send(o, i2, total(yp, None), v2.at[0], d_yp)
            send(o, i2, total(ym, None), v2.at[1], d_ym)

        def third():
            arrive(i2, v2)
            return total(y, None)[...] + v2[0] + v2[1]

        return first, second, third

    def d_slice(i):
        n = PIECES[i][1] - PIECES[i][0]

        def total(t, h):
            units = pl.ds(0, n) if h is None else pl.ds(h * (n // 2), n // 2)
            return dpart[i].at[units, c, pl.ds(pl.multiple_of(t * srow, 16), srow)]

        return total

    o_dr = new_s()
    d_ring = [scatter(o_dr, d_slice(i), r1[i], r2[i]) for i in range(NP)]

    def d_first(i):
        arrive(i_dc[i], dcore[i])
        dpart[i][:, c] = dpart[i][:, c] + dcore[i][...]
        d_ring[i][0]()

    o_k, i_k = new_s(), [new() for _ in range(4)]
    k_to = (d_xp, d_xm, d_x2, d_sib)

    def d_third(i):
        dist = d_ring[i][2]()
        val = jnp.exp(dist * (-inv_f)).astype(BF16)
        lo, hi, s = PIECES[i]
        for j in range(hi - lo):
            k, r = UNITS[lo + j]
            ref = kx.at[x, c, s, pl.ds(pl.multiple_of((xabs[k] * 2 + r) * srow, 16), srow)]
            ref[...] = val[j]
            for n, to in enumerate(k_to):
                send(o_k, i_k[n], ref, ref, to)

    arrive(i_sc, z_piece(1, 0))
    z_step(1, 0)
    pl.semaphore_wait(hello.at[0], len(near))
    greet(hello.at[1], near)
    z_step(0, 2)
    x_pass(0, 0)
    x_pass(1, 0)
    pl.semaphore_wait(hello.at[1], len(near))
    w_start()
    arrive(i_sp[0], px.at[UNIT[OWN, 0], oh])
    x_own(0, 1, 0)
    z_step(1, 2)
    arrive(i_sp[1], px.at[UNIT[OWN, 1], oh])
    x_own(0, 1, 1)
    x_own(1, 1, 1)
    x_own(1, 1, 0)
    z_step(0, 4)
    for cp in loads:
        cp.wait()
    z_step(1, 4)
    x_pass(0, 1)
    x_pass(1, 1)
    arrive(i_near, cx.at[0:4])
    set_ready(0)
    tiles(0)
    z_step(0, 6)
    z_step(1, 6)
    arrive(i_w, wx.at[0])
    z_step(2, 0)
    arrive(i_xo[0], px.at[0])
    tiles(1)
    d_first(0)
    d_first(1)
    arrive(i_far, cx.at[0:5])
    set_ready(1)
    tiles(3)
    d_ring[0][1]()
    arrive(i_xo[1], px.at[0])
    arrive(i_xf, px.at[6:8])
    tiles(2)
    d_first(3)
    tiles(4)
    d_ring[1][1]()
    z_step(2, 2)
    d_first(2)
    d_first(4)
    d_ring[3][1]()
    d_third(0)
    d_third(1)
    d_ring[2][1]()
    z_step(2, 4)
    d_ring[4][1]()
    d_third(3)
    d_third(2)
    z_step(2, 6)
    d_third(4)

    for n, xs in enumerate((xm, xp, x2)):
        arrive(i_k[n], kx.at[xs, c])
        send(o_k, i_k[3], kx.at[xs, c], kx.at[xs, c], d_sib)

    def fit_of(cc):
        fit = None
        for xs in range(NX):
            for s in range(2):
                w = wx[s * HALF : (s + 1) * HALF, xs].reshape(cset, lab)
                term = jnp.dot(kx[xs, cc, s], w, preferred_element_type=F32)
                fit = term if fit is None else fit + term
        return fit.astype(BF16)

    def keep(cc):
        fitted[pl.ds(pl.multiple_of(cc * 2 * hrow, 16), 2 * hrow)] = fit_of(cc)

    arrive(i_wrest, wx.at[0:9])
    keep(c)
    arrive(i_k[3], kx.at[:, 1 - c])
    keep(1 - c)

    for y_ in (y2, yp, ym, y):
        for s in range(2):
            kk = kx[y_, :, s].reshape(4 * hrow, cset)
            gsum[y_, s * cset : (s + 1) * cset] = lax.dot_general(
                kk, fitted[...], (((0,), (0,)), ((), ())), preferred_element_type=F32
            )

    grow = 2 * cset // 4
    zper = NZ // 4
    o_g, o_za, o_zn, o_z1, o_z0 = (new_s() for _ in range(5))
    i_za, i_zn, i_z0 = new(), new(), [new(), new()]
    own = jnp.logical_and(diag, y == x)

    def g_rows(rel, yy=None):
        slot = SLOT[rel]
        if yy is None:
            return gout.at[slot * 2 * crow : (slot + 1) * 2 * crow]
        return gout.at[pl.ds(pl.multiple_of((2 * slot + yy) * crow, 16), crow)]

    def z_final(rel, n):
        yy = yh ^ n
        out_sem = o_zn if rel else (o_z0, o_z1)[n]
        j = NEAR.index(rel)
        to = dev(yh_=yy, x_=y, z_=zat(rel), q_=x)
        src = g_rows(rel, yy)
        if rel:
            return copy(out_sem, i_zn, src, zb.at[c, j], to)
        return pltpu.make_async_remote_copy(
            src_ref=src, dst_ref=zb.at[c, j], send_sem=ssem.at[out_sem], recv_sem=rsem.at[i_z0[0] + c],
            device_id=to, device_id_type=MESH,
        )

    def z0_arrive(cc):
        ref = zb.at[cc, 0]
        pltpu.make_async_remote_copy(
            src_ref=ref, dst_ref=ref, send_sem=ssem.at[o_z0], recv_sem=rsem.at[i_z0[0] + cc],
            device_id=d_sib, device_id_type=MESH,
        ).wait_recv()

    def z_relay(rel):
        if rel == HALF:
            for d in range(2):
                rows = pl.ds(d * crow, crow)
                src = gout.at[pl.ds((2 * SLOT[rel] + d) * crow, crow)]
                send(o_za, i_za, src, za.at[6, rows], dev(z_=zat(4 * sign[d])))
            return
        d = 0 if rel > 0 else 1
        hop = abs(rel) - 4
        send(o_za, i_za, g_rows(rel), za.at[2 * (hop - 1) + d], dev(z_=zat(sign[d] * hop)))

    def g_slice(p):
        def total(t, h):
            lo, num = (0, grow) if h is None else (h * (grow // 2), grow // 2)
            return gsum.at[t, pl.ds(p * grow + lo, num)]

        return total

    order = (3, 2, 1, 0)
    g_ring = [scatter(o_g, g_slice(p), g1.at[p], g2.at[p]) for p in range(4)]
    for stage in range(2):
        for p in order:
            g_ring[p][stage]()
    for p in order:
        gout[p * grow : (p + 1) * grow] = g_ring[p][2]()
        for rel in reversed(REL[p * zper : (p + 1) * zper]):
            if abs(rel) > 4:
                z_relay(rel)
            elif rel and abs(rel) < 4:
                for n in range(2):
                    z_final(rel, n).start()
    z_final(0, 1).start()

    @pl.when(own)
    def _():
        zb[c, 0] = g_rows(0, yh)[...]

    arrive(i_za, za)
    for d, rel in enumerate((4, -4)):
        ref = g_rows(rel)
        ref[...] = ref[...] + za[d] + za[2 + d] + za[4 + d]
        part = gout.at[pl.ds((2 * SLOT[rel] + d) * crow, crow)]
        part[...] = part[...] + za[6, d * crow : (d + 1) * crow]
        for n in range(2):
            z_final(rel, n).start()

    @pl.when(jnp.logical_not(own))
    def _():
        z_final(0, 0).start()
        z0_arrive(c)

    z0_arrive(1 - c)
    arrive(i_zn, zb.at[:, 1:])
    for cc in range(2):
        total = zb[cc, 0]
        for j in range(1, len(NEAR)):
            total = total + zb[cc, j]
        out[:, cc * lab : (cc + 1) * lab] = total * scale

    assert used == [SENDS, ARRIVALS], used
    sent(o_z, cx.at[0 : NZ - 1])
    sent(o_zw, wx.at[0 : NZ - 1])
    sent(o_sc, cx.at[0, 0])
    sent(o_x, px.at[0:6])
    sent(o_sp, px.at[0])
    sent(o_w, wx.at[0:7, 0, 0])
    sent(o_dc, cx)
    sent(o_dr, px.at[0:3])
    sent(o_k, cx.at[0:14])
    sent(o_g, px.at[0:3])
    sent(o_za, za)
    sent(o_zn, zb.at[:, 1:])
    sent(o_z1, zb.at[0, 0])

    @pl.when(jnp.logical_not(diag))
    def _():
        sent(o_w0, wx.at[0, 0, 0])

    @pl.when(jnp.logical_not(own))
    def _():
        sent(o_z0, zb.at[0, 0])


def solution(mesh):
    assert mesh.shape["blk"] == 2 * NX * NZ and mesh.shape["feat"] == 4

    def step(points, centers, coefs):
        rows, qf = points.shape
        crow, labels = coefs.shape
        feats, cset, lab = qf // 2, 2 * HALF * crow, labels // 2
        npts = rows * mesh.shape["blk"]
        nf = qf * mesh.shape["feat"]
        srow, grow, cols = rows // 2 // NY, 2 * cset // 4, cset
        V = pltpu.VMEM
        per_piece = [
            [V(shape(hi - lo), F32) for lo, hi, _ in PIECES]
            for shape in (
                lambda n: (n, 2, rows // 2, cols),
                lambda n: (n, rows // 2, cols),
                lambda n: (2, n // 2, srow, cols),
                lambda n: (2, n, srow, cols),
            )
        ]
        return pl.pallas_call(
            functools.partial(kernel, 1.0 / nf, 1.0 / math.sqrt(npts)),
            out_shape=jax.ShapeDtypeStruct((crow, labels), F32),
            in_specs=[pl.BlockSpec(memory_space=pl.ANY)] * 3,
            out_specs=pl.BlockSpec(memory_space=pltpu.VMEM),
            scratch_shapes=[
                V((2 * NX, 2, rows // 2, feats), BF16),
                V((NZ, 2, crow, feats), BF16),
                V((NZ, NX, 2, crow, lab), BF16),
                V((NX, 2, 2, rows, cset), BF16),
                V((4, 2 * cset, lab), F32),
                V((2 * cset, lab), F32),
                V((2, len(NEAR), crow, lab), F32),
                V((4, 2, grow // 2, lab), F32),
                V((4, 2, grow, lab), F32),
                V((7, 2 * crow, lab), F32),
                V((8 * rows, 1), F32),
                V((2 * rows, lab), BF16),
                *[v for group in per_piece for v in group],
                pltpu.SemaphoreType.DMA((SENDS,)),
                pltpu.SemaphoreType.DMA((ARRIVALS,)),
                pltpu.SemaphoreType.DMA((3,)),
                pltpu.SemaphoreType.REGULAR((2,)),
            ],
            compiler_params=pltpu.CompilerParams(collective_id=0, has_side_effects=True),
        )(points, centers, coefs)

    spec = P("blk", "feat")
    return jax.shard_map(
        step, mesh=mesh, in_specs=(spec, spec, spec), out_specs=spec, check_vma=False
    )
```

```python
import functools
import math

import jax
import jax.numpy as jnp
from jax import lax
from jax.experimental import pallas as pl
from jax.experimental.pallas import tpu as pltpu
from jax.sharding import PartitionSpec as P

MESH = pl.DeviceIdType.MESH
F32, BF16 = jnp.float32, jnp.bfloat16
NX, NY, NZ = 4, 4, 16
SENDS, ARRIVALS = 15, 63
REL = [0] + [s * d for d in range(1, NZ // 2) for s in (1, -1)] + [NZ // 2]
REL.remove(4), REL.insert(7, 4)
SLOT = {r: i for i, r in enumerate(REL)}
HALF = NZ // 2
OWN, LEFT, RIGHT, FAR = range(4)
UNITS = ((OWN, 0), (OWN, 1), (LEFT, 0), (RIGHT, 1), (LEFT, 1), (RIGHT, 0), (FAR, 0), (FAR, 1))
UNIT = {u: i for i, u in enumerate(UNITS)}
PIECES = ((0, 2, 0), (2, 4, 0), (4, 6, 0), (6, 8, 0), (0, 4, 1), (4, 8, 1))
NEAR = [0, 1, -1, 2, -2, 3, -3, 4, -4]
NP = len(PIECES)
STOPS = ((0, 2, 4, 6, 8),) * 3


def kernel(
    inv_f, scale, pts, ctr, wts, out,
    px, cx, wx, kx, gsum, gout, zb, *rest,
):
    g1, g2, za, psq, fitted = rest[:5]
    dpart, dcore, r1, r2 = (rest[5 + NP * i : 5 + NP * (i + 1)] for i in range(4))
    ssem, rsem, lsem, hello = rest[5 + 4 * NP :]
    b, q = lax.axis_index("blk"), lax.axis_index("feat")
    yh, x, z = b // (NX * NZ), (b // NZ) % NX, b % NZ
    yl, c = q // 2, q % 2
    y, oh = 2 * yh + yl, 1 - yh
    feats = pts.shape[1] // 2
    hrow = pts.shape[0] // 2
    crow = ctr.shape[0]
    cset = 2 * HALF * crow
    lab = wts.shape[1] // 2

    def dev(yh_=None, x_=None, z_=None, q_=None):
        yh_ = yh if yh_ is None else yh_
        x_ = x if x_ is None else x_
        z_ = z if z_ is None else z_
        return ((yh_ * NX + x_) * NZ + z_, q if q_ is None else q_)

    def ydev(y_):
        return dev(yh_=y_ // 2, q_=(y_ % 2) * 2 + c)

    def zat(rel):
        return (z + rel + NZ) % NZ

    xp, xm, x2 = (x + 1) % NX, (x + 3) % NX, (x + 2) % NX
    xabs = (x, xm, xp, x2)
    yp, ym, y2 = (y + 1) % NY, (y + 3) % NY, (y + 2) % NY
    d_xp, d_xm, d_x2 = dev(x_=xp), dev(x_=xm), dev(x_=x2)
    d_yp, d_ym, d_y2 = ydev(yp), ydev(ym), ydev(y2)
    d_sib = dev(q_=2 * yl + 1 - c)
    diag = x == q

    used = [0, 0]

    def counter(which, limit):
        def new():
            used[which] += 1
            assert used[which] <= limit
            return used[which] - 1
        return new

    new_s, new = counter(0, SENDS), counter(1, ARRIVALS)

    def copy(o, i, src, dst, to):
        return pltpu.make_async_remote_copy(
            src_ref=src, dst_ref=dst, send_sem=ssem.at[o], recv_sem=rsem.at[i],
            device_id=to, device_id_type=MESH,
        )

    def send(o, i, src, dst, to):
        copy(o, i, src, dst, to).start()

    def arrive(i, ref):
        copy(0, i, ref, ref, d_sib).wait_recv()

    def sent(o, ref):
        copy(o, 0, ref, ref, d_sib).wait_send()

    def half(ref, h, lo=0, num=None):
        num = ref.shape[0] if num is None else num
        return ref.at[pl.ds(lo, num), pl.ds(pl.multiple_of(h * feats, 128), feats)]

    def ctr_at(yh_, rel):
        return cx.at[SLOT[HALF if rel == -HALF else rel], yh_]

    def z_piece(kind, rel):
        if kind == 2:
            return wx.at[SLOT[HALF if rel == -HALF else rel]]
        return ctr_at(oh if kind == 1 else yh, rel)

    loads = [pltpu.make_async_copy(half(ctr, yh), z_piece(0, 0), lsem.at[0])]
    loads += [
        pltpu.make_async_copy(half(pts, yh, r * hrow, hrow), px.at[UNIT[OWN, r], yh], lsem.at[1 + r])
        for r in range(2)
    ]
    for cp in loads:
        cp.start()

    barrier = pltpu.get_barrier_semaphore()
    near = [dev(z_=zat(r)) for r in (1, -1, 2, -2)] + [d_xp, d_xm, d_x2, d_yp, d_ym, d_y2, d_sib]
    w_to = [dev(yh_=(y + n) % NY // 2, x_=q, q_=(y + n) % NY % 2 * 2 + cc) for n in range(NY) for cc in (c, 1 - c)]

    def greet(sem, others):
        for other in others:
            pl.semaphore_signal(sem, inc=1, device_id=other, device_id_type=MESH)

    greet(barrier, near)
    pl.semaphore_wait(barrier, len(near))
    greet(hello.at[0], near)

    o_z, o_zw = new_s(), new_s()
    PARTS = 2
    PARTS = 2
    i_step = [{n: [new() for _ in range(PARTS if kind < 2 else 1)] for n in STOPS[kind][1:-1]} for kind in range(3)]
    i_near, i_far, i_wrest = new(), new(), new()
    sign = (1, -1)

    def z_there(d, kind, dist):
        return dist < HALF or (kind == 1) == (d == 1)

    def z_part(ref, part):
        return ref.at[:, part * (feats // PARTS) : (part + 1) * (feats // PARTS)]

    def z_send(d, kind, dist, hop, part=None, src=None):
        if not z_there(d, kind, dist + hop):
            return
        src = z_piece(kind, -sign[d] * dist) if src is None else src
        dst = z_piece(kind, -sign[d] * (dist + hop))
        if dist + hop in i_step[kind]:
            i = i_step[kind][dist + hop][part or 0]
        elif kind == 2:
            i = i_wrest
        else:
            i = i_near if dist + hop < 4 else i_far
        if part is not None:
            src, dst = z_part(src, part), z_part(dst, part)
        send(o_zw if kind == 2 else o_z, i, src, dst, dev(z_=zat(hop * sign[d])))

    def z_step(kind, dist, src=None):
        last = STOPS[kind][STOPS[kind].index(dist) + 1] - dist
        for part in range(PARTS if kind < 2 else 1):
            if dist:
                arrive(i_step[kind][dist][part], wx.at[0:2] if kind == 2 else cx.at[0, 0])
            for d in range(2):
                z_send(d, kind, dist, last, part if kind < 2 else None, src)
        for hop in range(last - 1, 0, -1):
            for d in range(2):
                z_send(d, kind, dist, hop, src=src)

    o_sc, i_sc = new_s(), new()
    send(o_sc, i_sc, half(ctr, oh), ctr_at(yh, 0), d_y2)
    z_step(0, 0, half(ctr, yh))

    o_x, o_sp = new_s(), new_s()
    i_sp = [new(), new()]
    i_x = [[new(), new()] for _ in range(2)]
    i_xo = [new(), new()]
    i_xf = new()
    x_to = ((d_xp, LEFT), (d_xm, RIGHT))

    def x_own(d, j, r, src=None):
        yy = oh if j else yh
        to, slot = x_to[d]
        src = px.at[UNIT[OWN, r], yy] if src is None else src
        send(o_x, i_x[d][j] if r == d else i_xo[j], src, px.at[UNIT[slot, r], yy], to)

    def x_pass(d, j):
        yy = oh if j else yh
        piece = px.at[UNIT[(LEFT, RIGHT)[d], d], yy]
        arrive(i_x[d][j], piece)
        send(o_x, i_xf, piece, px.at[UNIT[FAR, d], yy], x_to[d][0])

    for r in range(2):
        x_own(0, 0, r, half(pts, yh, r * hrow, hrow))
        x_own(1, 0, 1 - r, half(pts, yh, (1 - r) * hrow, hrow))
        send(o_sp, i_sp[r], half(pts, oh, r * hrow, hrow), px.at[UNIT[OWN, r], yh], d_y2)

    o_w, o_w0, i_w = new_s(), new_s(), new()

    def w_copy(n, local=False):
        src = wts.at[:, pl.ds(pl.multiple_of((c ^ (n % 2)) * lab, 128), lab)]
        if local:
            return pltpu.make_async_copy(src, wx.at[0, x, yh], rsem.at[i_w])
        return copy(o_w if n else o_w0, i_w, src, wx.at[0, x, yh], w_to[n])

    def w_start():
        for n in range(1, 8):
            w_copy(n).start()

        @pl.when(jnp.logical_not(diag))
        def _():
            w_copy(0).start()

        @pl.when(diag)
        def _():
            w_copy(0, True).start()

    def square(v):
        v = v.astype(F32)
        return jnp.sum(v * v, axis=1, keepdims=True)

    csq = [None, None]

    def centers(s):
        return cx[s * HALF : (s + 1) * HALF].reshape(cset, feats)

    def set_ready(s):
        sq = square(centers(s))
        csq[s] = jnp.transpose(jnp.broadcast_to(sq, (sq.shape[0], 128)))[0:1, :]

    srow = hrow // NY
    o_dc, i_dc = new_s(), [new() for _ in range(NP)]

    def tiles(i):
        lo, hi, s = PIECES[i]
        n = (hi - lo) * 2 * hrow
        p = px[lo:hi].reshape(n, feats)
        if s == 0:
            psq[lo * 2 * hrow : hi * 2 * hrow] = square(p)
        cross = lax.dot_general(p, centers(s), (((1,), (1,)), ((), ())), preferred_element_type=F32)
        part = psq[lo * 2 * hrow : hi * 2 * hrow] + csq[s] - 2.0 * cross
        dpart[i][...] = part.reshape(hi - lo, 2, hrow, cset)
        send(o_dc, i_dc[i], dpart[i].at[:, 1 - c], dcore[i], d_sib)

    def scatter(o, total, v1, v2):
        i1, i2 = new(), new()

        def first():
            send(o, i1, total(y2, 0), v1.at[0], d_yp)
            send(o, i1, total(y2, 1), v1.at[1], d_ym)

        def second():
            arrive(i1, v1)
            for h, y_ in enumerate((yp, ym)):
                ref = total(y_, h)
                ref[...] = ref[...] + v1[h]
            send(o, i2, total(yp, None), v2.at[0], d_yp)
            send(o, i2, total(ym, None), v2.at[1], d_ym)

        def third():
            arrive(i2, v2)
            return total(y, None)[...] + v2[0] + v2[1]

        return first, second, third

    def d_slice(i):
        n = PIECES[i][1] - PIECES[i][0]

        def total(t, h):
            units = pl.ds(0, n) if h is None else pl.ds(h * (n // 2), n // 2)
            return dpart[i].at[units, c, pl.ds(pl.multiple_of(t * srow, 16), srow)]

        return total

    o_dr = new_s()
    d_ring = [scatter(o_dr, d_slice(i), r1[i], r2[i]) for i in range(NP)]

    def d_first(i):
        arrive(i_dc[i], dcore[i])
        dpart[i][:, c] = dpart[i][:, c] + dcore[i][...]
        d_ring[i][0]()

    o_k, i_k = new_s(), [new() for _ in range(4)]
    k_to = (d_xp, d_xm, d_x2, d_sib)

    def d_third(i):
        dist = d_ring[i][2]()
        val = jnp.exp(dist * (-inv_f)).astype(BF16)
        lo, hi, s = PIECES[i]
        for j in range(hi - lo):
            k, r = UNITS[lo + j]
            ref = kx.at[x, c, s, pl.ds(pl.multiple_of((xabs[k] * 2 + r) * srow, 16), srow)]
            ref[...] = val[j]
            for n in (2, 0, 1, 3):
                send(o_k, i_k[n], ref, ref, k_to[n])

    arrive(i_sc, z_piece(1, 0))
    z_step(1, 0)
    pl.semaphore_wait(hello.at[0], len(near))
    greet(hello.at[1], near)
    z_step(0, 2)
    x_pass(0, 0)
    x_pass(1, 0)
    pl.semaphore_wait(hello.at[1], len(near))
    w_start()
    arrive(i_sp[0], px.at[UNIT[OWN, 0], oh])
    x_own(0, 1, 0)
    z_step(1, 2)
    arrive(i_sp[1], px.at[UNIT[OWN, 1], oh])
    x_own(0, 1, 1)
    x_own(1, 1, 1)
    x_own(1, 1, 0)
    z_step(0, 4)
    for cp in loads:
        cp.wait()
    z_step(1, 4)
    x_pass(0, 1)
    x_pass(1, 1)
    arrive(i_near, cx.at[0:4])
    set_ready(0)
    tiles(0)
    z_step(0, 6)
    z_step(1, 6)
    arrive(i_w, wx.at[0])
    z_step(2, 0)
    arrive(i_xo[0], px.at[0])
    tiles(1)
    d_first(0)
    arrive(i_xo[1], px.at[0])
    tiles(2)
    d_first(1)
    d_ring[0][1]()
    arrive(i_xf, px.at[6:8])
    tiles(3)
    d_first(2)
    arrive(i_far, cx.at[0:5])
    set_ready(1)
    tiles(4)
    d_first(3)
    d_ring[1][1]()
    tiles(5)
    d_first(4)
    d_ring[2][1]()
    z_step(2, 2)
    d_first(5)
    d_ring[3][1]()
    d_third(0)
    d_third(1)
    d_third(2)
    d_ring[4][1]()
    z_step(2, 4)
    d_ring[5][1]()
    d_third(3)
    d_third(4)
    z_step(2, 6)
    d_third(5)

    for n, xs in enumerate((xm, xp, x2)):
        arrive(i_k[n], kx.at[xs, c])
        send(o_k, i_k[3], kx.at[xs, c], kx.at[xs, c], d_sib)

    def fit_of(cc):
        fit = None
        for xs in range(NX):
            for s in range(2):
                w = wx[s * HALF : (s + 1) * HALF, xs].reshape(cset, lab)
                term = jnp.dot(kx[xs, cc, s], w, preferred_element_type=F32)
                fit = term if fit is None else fit + term
        return fit.astype(BF16)

    def keep(cc):
        fitted[pl.ds(pl.multiple_of(cc * 2 * hrow, 16), 2 * hrow)] = fit_of(cc)

    arrive(i_wrest, wx.at[0:9])
    keep(c)
    arrive(i_k[3], kx.at[:, 1 - c])
    keep(1 - c)

    grow = 2 * cset // 4
    zper = NZ // 4
    o_g, o_za, o_zn, o_z1, o_z0 = (new_s() for _ in range(5))
    i_za, i_zn, i_z0 = new(), new(), [new(), new()]
    own = jnp.logical_and(diag, y == x)

    def g_rows(rel, yy=None):
        slot = SLOT[rel]
        if yy is None:
            return gout.at[slot * 2 * crow : (slot + 1) * 2 * crow]
        return gout.at[pl.ds(pl.multiple_of((2 * slot + yy) * crow, 16), crow)]

    def z_final(rel, n):
        yy = yh ^ n
        out_sem = o_zn if rel else (o_z0, o_z1)[n]
        j = NEAR.index(rel)
        to = dev(yh_=yy, x_=y, z_=zat(rel), q_=x)
        src = g_rows(rel, yy)
        if rel:
            return copy(out_sem, i_zn, src, zb.at[c, j], to)
        return pltpu.make_async_remote_copy(
            src_ref=src, dst_ref=zb.at[c, j], send_sem=ssem.at[out_sem], recv_sem=rsem.at[i_z0[0] + c],
            device_id=to, device_id_type=MESH,
        )

    def z0_arrive(cc):
        ref = zb.at[cc, 0]
        pltpu.make_async_remote_copy(
            src_ref=ref, dst_ref=ref, send_sem=ssem.at[o_z0], recv_sem=rsem.at[i_z0[0] + cc],
            device_id=d_sib, device_id_type=MESH,
        ).wait_recv()

    def z_relay(rel):
        if rel == HALF:
            for d in range(2):
                rows = pl.ds(d * crow, crow)
                src = gout.at[pl.ds((2 * SLOT[rel] + d) * crow, crow)]
                send(o_za, i_za, src, za.at[6, rows], dev(z_=zat(4 * sign[d])))
            return
        d = 0 if rel > 0 else 1
        hop = abs(rel) - 4
        send(o_za, i_za, g_rows(rel), za.at[2 * (hop - 1) + d], dev(z_=zat(sign[d] * hop)))

    def g_slice(p):
        def total(t, h):
            lo, num = (0, grow) if h is None else (h * (grow // 2), grow // 2)
            return gsum.at[t, pl.ds(p * grow + lo, num)]

        return total

    order = (3, 2, 1, 0)
    g_ring = [scatter(o_g, g_slice(p), g1.at[p], g2.at[p]) for p in range(4)]
    for s in (1, 0):
        for y_ in (y2, yp, ym, y):
            kk = kx[y_, :, s].reshape(4 * hrow, cset)
            gsum[y_, s * cset : (s + 1) * cset] = lax.dot_general(
                kk, fitted[...], (((0,), (0,)), ((), ())), preferred_element_type=F32
            )
        for p in order[2 - 2 * s : 4 - 2 * s]:
            g_ring[p][0]()
    for p in order:
        g_ring[p][1]()
    for p in order:
        gout[p * grow : (p + 1) * grow] = g_ring[p][2]()
        for rel in reversed(REL[p * zper : (p + 1) * zper]):
            if abs(rel) > 4:
                z_relay(rel)
            elif rel and abs(rel) < 4:
                for n in range(2):
                    z_final(rel, n).start()
    z_final(0, 1).start()

    @pl.when(own)
    def _():
        zb[c, 0] = g_rows(0, yh)[...]

    arrive(i_za, za)
    for d, rel in enumerate((4, -4)):
        ref = g_rows(rel)
        ref[...] = ref[...] + za[d] + za[2 + d] + za[4 + d]
        part = gout.at[pl.ds((2 * SLOT[rel] + d) * crow, crow)]
        part[...] = part[...] + za[6, d * crow : (d + 1) * crow]
        for n in range(2):
            z_final(rel, n).start()

    @pl.when(jnp.logical_not(own))
    def _():
        z_final(0, 0).start()
        z0_arrive(c)

    z0_arrive(1 - c)
    arrive(i_zn, zb.at[:, 1:])
    for cc in range(2):
        total = zb[cc, 0]
        for j in range(1, len(NEAR)):
            total = total + zb[cc, j]
        out[:, cc * lab : (cc + 1) * lab] = total * scale

    assert used == [SENDS, ARRIVALS], used
    sent(o_z, cx.at[0 : NZ - 1])
    sent(o_zw, wx.at[0 : NZ - 1])
    sent(o_sc, cx.at[0, 0])
    sent(o_x, px.at[0:6])
    sent(o_sp, px.at[0])
    sent(o_w, wx.at[0:7, 0, 0])
    sent(o_dc, cx)
    sent(o_dr, px.at[0:3])
    sent(o_k, cx.at[0:14])
    sent(o_g, px.at[0:3])
    sent(o_za, za)
    sent(o_zn, zb.at[:, 1:])
    sent(o_z1, zb.at[0, 0])

    @pl.when(jnp.logical_not(diag))
    def _():
        sent(o_w0, wx.at[0, 0, 0])

    @pl.when(jnp.logical_not(own))
    def _():
        sent(o_z0, zb.at[0, 0])


def solution(mesh):
    assert mesh.shape["blk"] == 2 * NX * NZ and mesh.shape["feat"] == 4

    def step(points, centers, coefs):
        rows, qf = points.shape
        crow, labels = coefs.shape
        feats, cset, lab = qf // 2, 2 * HALF * crow, labels // 2
        npts = rows * mesh.shape["blk"]
        nf = qf * mesh.shape["feat"]
        srow, grow, cols = rows // 2 // NY, 2 * cset // 4, cset
        V = pltpu.VMEM
        per_piece = [
            [V(shape(hi - lo), F32) for lo, hi, _ in PIECES]
            for shape in (
                lambda n: (n, 2, rows // 2, cols),
                lambda n: (n, rows // 2, cols),
                lambda n: (2, n // 2, srow, cols),
                lambda n: (2, n, srow, cols),
            )
        ]
        return pl.pallas_call(
            functools.partial(kernel, 1.0 / nf, 1.0 / math.sqrt(npts)),
            out_shape=jax.ShapeDtypeStruct((crow, labels), F32),
            in_specs=[pl.BlockSpec(memory_space=pl.ANY)] * 3,
            out_specs=pl.BlockSpec(memory_space=pltpu.VMEM),
            scratch_shapes=[
                V((2 * NX, 2, rows // 2, feats), BF16),
                V((NZ, 2, crow, feats), BF16),
                V((NZ, NX, 2, crow, lab), BF16),
                V((NX, 2, 2, rows, cset), BF16),
                V((4, 2 * cset, lab), F32),
                V((2 * cset, lab), F32),
                V((2, len(NEAR), crow, lab), F32),
                V((4, 2, grow // 2, lab), F32),
                V((4, 2, grow, lab), F32),
                V((7, 2 * crow, lab), F32),
                V((8 * rows, 1), F32),
                V((2 * rows, lab), BF16),
                *[v for group in per_piece for v in group],
                pltpu.SemaphoreType.DMA((SENDS,)),
                pltpu.SemaphoreType.DMA((ARRIVALS,)),
                pltpu.SemaphoreType.DMA((3,)),
                pltpu.SemaphoreType.REGULAR((2,)),
            ],
            compiler_params=pltpu.CompilerParams(collective_id=0, has_side_effects=True),
        )(points, centers, coefs)

    spec = P("blk", "feat")
    return jax.shard_map(
        step, mesh=mesh, in_specs=(spec, spec, spec), out_specs=spec, check_vma=False
    )
```

```python
import functools
import math

import jax
import jax.numpy as jnp
from jax import lax
from jax.experimental import pallas as pl
from jax.experimental.pallas import tpu as pltpu
from jax.sharding import PartitionSpec as P

MESH = pl.DeviceIdType.MESH
F32, BF16 = jnp.float32, jnp.bfloat16
NX, NY, NZ = 4, 4, 16
SENDS, ARRIVALS = 15, 63
REL = [0] + [s * d for d in range(1, NZ // 2) for s in (1, -1)] + [NZ // 2]
REL.remove(4), REL.insert(7, 4)
SLOT = {r: i for i, r in enumerate(REL)}
HALF = NZ // 2
OWN, LEFT, RIGHT, FAR = range(4)
UNITS = ((OWN, 0), (OWN, 1), (LEFT, 0), (RIGHT, 1), (LEFT, 1), (RIGHT, 0), (FAR, 0), (FAR, 1))
UNIT = {u: i for i, u in enumerate(UNITS)}
PIECES = ((0, 2, 0), (2, 4, 0), (4, 6, 0), (6, 8, 0), (0, 4, 1), (4, 8, 1))
NEAR = [0, 1, -1, 2, -2, 3, -3, 4, -4]
NP = len(PIECES)
STOPS = ((0, 2, 4, 6, 8),) * 3


def kernel(
    inv_f, scale, pts, ctr, wts, out,
    px, cx, wx, kx, gsum, gout, zb, *rest,
):
    g1, g2, za, psq, fitted = rest[:5]
    dpart, dcore, r1, r2 = (rest[5 + NP * i : 5 + NP * (i + 1)] for i in range(4))
    ssem, rsem, lsem, hello = rest[5 + 4 * NP :]
    b, q = lax.axis_index("blk"), lax.axis_index("feat")
    yh, x, z = b // (NX * NZ), (b // NZ) % NX, b % NZ
    yl, c = q // 2, q % 2
    y, oh = 2 * yh + yl, 1 - yh
    feats = pts.shape[1] // 2
    hrow = pts.shape[0] // 2
    crow = ctr.shape[0]
    cset = 2 * HALF * crow
    lab = wts.shape[1] // 2

    def dev(yh_=None, x_=None, z_=None, q_=None):
        yh_ = yh if yh_ is None else yh_
        x_ = x if x_ is None else x_
        z_ = z if z_ is None else z_
        return ((yh_ * NX + x_) * NZ + z_, q if q_ is None else q_)

    def ydev(y_):
        return dev(yh_=y_ // 2, q_=(y_ % 2) * 2 + c)

    def zat(rel):
        return (z + rel + NZ) % NZ

    xp, xm, x2 = (x + 1) % NX, (x + 3) % NX, (x + 2) % NX
    xabs = (x, xm, xp, x2)
    yp, ym, y2 = (y + 1) % NY, (y + 3) % NY, (y + 2) % NY
    d_xp, d_xm, d_x2 = dev(x_=xp), dev(x_=xm), dev(x_=x2)
    d_yp, d_ym, d_y2 = ydev(yp), ydev(ym), ydev(y2)
    d_sib = dev(q_=2 * yl + 1 - c)
    diag = x == q

    used = [0, 0]

    def counter(which, limit):
        def new():
            used[which] += 1
            assert used[which] <= limit
            return used[which] - 1
        return new

    new_s, new = counter(0, SENDS), counter(1, ARRIVALS)

    def copy(o, i, src, dst, to):
        return pltpu.make_async_remote_copy(
            src_ref=src, dst_ref=dst, send_sem=ssem.at[o], recv_sem=rsem.at[i],
            device_id=to, device_id_type=MESH,
        )

    def send(o, i, src, dst, to):
        copy(o, i, src, dst, to).start()

    def arrive(i, ref):
        copy(0, i, ref, ref, d_sib).wait_recv()

    def sent(o, ref):
        copy(o, 0, ref, ref, d_sib).wait_send()

    def half(ref, h, lo=0, num=None):
        num = ref.shape[0] if num is None else num
        return ref.at[pl.ds(lo, num), pl.ds(pl.multiple_of(h * feats, 128), feats)]

    def ctr_at(yh_, rel):
        return cx.at[SLOT[HALF if rel == -HALF else rel], yh_]

    def z_piece(kind, rel):
        if kind == 2:
            return wx.at[SLOT[HALF if rel == -HALF else rel]]
        return ctr_at(oh if kind == 1 else yh, rel)

    loads = [pltpu.make_async_copy(half(ctr, yh), z_piece(0, 0), lsem.at[0])]
    loads += [
        pltpu.make_async_copy(half(pts, yh, r * hrow, hrow), px.at[UNIT[OWN, r], yh], lsem.at[1 + r])
        for r in range(2)
    ]
    for cp in loads:
        cp.start()

    barrier = pltpu.get_barrier_semaphore()
    near = [dev(z_=zat(r)) for r in (1, -1, 2, -2)] + [d_xp, d_xm, d_x2, d_yp, d_ym, d_y2, d_sib]
    w_to = [dev(yh_=(y + n) % NY // 2, x_=q, q_=(y + n) % NY % 2 * 2 + cc) for n in range(NY) for cc in (c, 1 - c)]

    def greet(sem, others):
        for other in others:
            pl.semaphore_signal(sem, inc=1, device_id=other, device_id_type=MESH)

    greet(barrier, near)
    pl.semaphore_wait(barrier, len(near))
    greet(hello.at[0], near)

    o_z, o_zw = new_s(), new_s()
    PARTS = 2
    PARTS = 2
    i_step = [{n: [new() for _ in range(PARTS if kind < 2 else 1)] for n in STOPS[kind][1:-1]} for kind in range(3)]
    i_near, i_far, i_wrest = new(), new(), new()
    sign = (1, -1)

    def z_there(d, kind, dist):
        return dist < HALF or (kind == 1) == (d == 1)

    def z_part(ref, part):
        return ref.at[:, part * (feats // PARTS) : (part + 1) * (feats // PARTS)]

    def z_send(d, kind, dist, hop, part=None, src=None):
        if not z_there(d, kind, dist + hop):
            return
        src = z_piece(kind, -sign[d] * dist) if src is None else src
        dst = z_piece(kind, -sign[d] * (dist + hop))
        if dist + hop in i_step[kind]:
            i = i_step[kind][dist + hop][part or 0]
        elif kind == 2:
            i = i_wrest
        else:
            i = i_near if dist + hop < 4 else i_far
        if part is not None:
            src, dst = z_part(src, part), z_part(dst, part)
        send(o_zw if kind == 2 else o_z, i, src, dst, dev(z_=zat(hop * sign[d])))

    def z_step(kind, dist, src=None):
        last = STOPS[kind][STOPS[kind].index(dist) + 1] - dist
        for part in range(PARTS if kind < 2 else 1):
            if dist:
                arrive(i_step[kind][dist][part], wx.at[0:2] if kind == 2 else cx.at[0, 0])
            for d in range(2):
                z_send(d, kind, dist, last, part if kind < 2 else None, src)
        for hop in range(last - 1, 0, -1):
            for d in range(2):
                z_send(d, kind, dist, hop, src=src)

    o_sc, i_sc = new_s(), new()
    send(o_sc, i_sc, half(ctr, oh), ctr_at(yh, 0), d_y2)
    z_step(0, 0, half(ctr, yh))

    o_x, o_sp = new_s(), new_s()
    i_sp = [new(), new()]
    i_x = [[new(), new()] for _ in range(2)]
    i_xo = [new(), new()]
    i_xf = new()
    x_to = ((d_xp, LEFT), (d_xm, RIGHT))

    def x_own(d, j, r, src=None):
        yy = oh if j else yh
        to, slot = x_to[d]
        src = px.at[UNIT[OWN, r], yy] if src is None else src
        send(o_x, i_x[d][j] if r == d else i_xo[j], src, px.at[UNIT[slot, r], yy], to)

    def x_pass(d, j):
        yy = oh if j else yh
        piece = px.at[UNIT[(LEFT, RIGHT)[d], d], yy]
        arrive(i_x[d][j], piece)
        send(o_x, i_xf, piece, px.at[UNIT[FAR, d], yy], x_to[d][0])

    for r in range(2):
        x_own(0, 0, r, half(pts, yh, r * hrow, hrow))
        x_own(1, 0, 1 - r, half(pts, yh, (1 - r) * hrow, hrow))
        send(o_sp, i_sp[r], half(pts, oh, r * hrow, hrow), px.at[UNIT[OWN, r], yh], d_y2)

    o_w, o_w0, i_w = new_s(), new_s(), new()

    def w_copy(n, local=False):
        src = wts.at[:, pl.ds(pl.multiple_of((c ^ (n % 2)) * lab, 128), lab)]
        if local:
            return pltpu.make_async_copy(src, wx.at[0, x, yh], rsem.at[i_w])
        return copy(o_w if n else o_w0, i_w, src, wx.at[0, x, yh], w_to[n])

    def w_start():
        for n in range(1, 8):
            w_copy(n).start()

        @pl.when(jnp.logical_not(diag))
        def _():
            w_copy(0).start()

        @pl.when(diag)
        def _():
            w_copy(0, True).start()

    def square(v):
        v = v.astype(F32)
        return jnp.sum(v * v, axis=1, keepdims=True)

    csq = [None, None]

    def centers(s):
        return cx[s * HALF : (s + 1) * HALF].reshape(cset, feats)

    def set_ready(s):
        sq = square(centers(s))
        csq[s] = jnp.transpose(jnp.broadcast_to(sq, (sq.shape[0], 128)))[0:1, :]

    srow = hrow // NY
    o_dc, i_dc = new_s(), [new() for _ in range(NP)]

    def tiles(i):
        lo, hi, s = PIECES[i]
        n = (hi - lo) * 2 * hrow
        p = px[lo:hi].reshape(n, feats)
        if s == 0:
            psq[lo * 2 * hrow : hi * 2 * hrow] = square(p)
        cross = lax.dot_general(p, centers(s), (((1,), (1,)), ((), ())), preferred_element_type=F32)
        part = psq[lo * 2 * hrow : hi * 2 * hrow] + csq[s] - 2.0 * cross
        dpart[i][...] = part.reshape(hi - lo, 2, hrow, cset)
        send(o_dc, i_dc[i], dpart[i].at[:, 1 - c], dcore[i], d_sib)

    def scatter(o, total, v1, v2):
        i1, i2 = new(), new()

        def first():
            send(o, i1, total(y2, 0), v1.at[0], d_yp)
            send(o, i1, total(y2, 1), v1.at[1], d_ym)

        def second():
            arrive(i1, v1)
            for h, y_ in enumerate((yp, ym)):
                ref = total(y_, h)
                ref[...] = ref[...] + v1[h]
            send(o, i2, total(yp, None), v2.at[0], d_yp)
            send(o, i2, total(ym, None), v2.at[1], d_ym)

        def third():
            arrive(i2, v2)
            return total(y, None)[...] + v2[0] + v2[1]

        return first, second, third

    def d_slice(i):
        n = PIECES[i][1] - PIECES[i][0]

        def total(t, h):
            units = pl.ds(0, n) if h is None else pl.ds(h * (n // 2), n // 2)
            return dpart[i].at[units, c, pl.ds(pl.multiple_of(t * srow, 16), srow)]

        return total

    o_dr = new_s()
    d_ring = [scatter(o_dr, d_slice(i), r1[i], r2[i]) for i in range(NP)]

    def d_first(i):
        arrive(i_dc[i], dcore[i])
        dpart[i][:, c] = dpart[i][:, c] + dcore[i][...]
        d_ring[i][0]()

    o_k, i_k = new_s(), [new() for _ in range(4)]
    k_to = (d_xp, d_xm, d_x2, d_sib)

    def d_third(i):
        dist = d_ring[i][2]()
        val = jnp.exp(dist * (-inv_f)).astype(BF16)
        lo, hi, s = PIECES[i]
        for j in range(hi - lo):
            k, r = UNITS[lo + j]
            ref = kx.at[x, c, s, pl.ds(pl.multiple_of((xabs[k] * 2 + r) * srow, 16), srow)]
            ref[...] = val[j]
            for n in (2, 0, 1, 3):
                send(o_k, i_k[n], ref, ref, k_to[n])

    arrive(i_sc, z_piece(1, 0))
    z_step(1, 0)
    pl.semaphore_wait(hello.at[0], len(near))
    greet(hello.at[1], near)
    z_step(0, 2)
    x_pass(0, 0)
    x_pass(1, 0)
    pl.semaphore_wait(hello.at[1], len(near))
    w_start()
    arrive(i_sp[0], px.at[UNIT[OWN, 0], oh])
    x_own(0, 1, 0)
    z_step(1, 2)
    arrive(i_sp[1], px.at[UNIT[OWN, 1], oh])
    x_own(0, 1, 1)
    x_own(1, 1, 1)
    x_own(1, 1, 0)
    z_step(0, 4)
    for cp in loads:
        cp.wait()
    z_step(1, 4)
    x_pass(0, 1)
    x_pass(1, 1)
    arrive(i_near, cx.at[0:4])
    set_ready(0)
    tiles(0)
    z_step(0, 6)
    z_step(1, 6)
    arrive(i_w, wx.at[0])
    z_step(2, 0)
    arrive(i_xo[0], px.at[0])
    tiles(1)
    d_first(0)
    arrive(i_xo[1], px.at[0])
    tiles(2)
    d_first(1)
    d_ring[0][1]()
    arrive(i_xf, px.at[6:8])
    tiles(3)
    d_first(2)
    arrive(i_far, cx.at[0:5])
    set_ready(1)
    tiles(4)
    d_first(3)
    d_ring[1][1]()
    tiles(5)
    d_first(4)
    d_ring[2][1]()
    z_step(2, 2)
    d_first(5)
    d_ring[3][1]()
    d_third(0)
    d_third(1)
    d_third(2)
    d_ring[4][1]()
    z_step(2, 4)
    d_ring[5][1]()
    d_third(3)
    d_third(4)
    z_step(2, 6)
    d_third(5)

    for n, xs in enumerate((xm, xp, x2)):
        arrive(i_k[n], kx.at[xs, c])
        send(o_k, i_k[3], kx.at[xs, c], kx.at[xs, c], d_sib)

    def fit_of(cc):
        fit = None
        for xs in range(NX):
            for s in range(2):
                w = wx[s * HALF : (s + 1) * HALF, xs].reshape(cset, lab)
                term = jnp.dot(kx[xs, cc, s], w, preferred_element_type=F32)
                fit = term if fit is None else fit + term
        return fit.astype(BF16)

    def keep(cc):
        fitted[pl.ds(pl.multiple_of(cc * 2 * hrow, 16), 2 * hrow)] = fit_of(cc)

    arrive(i_wrest, wx.at[0:9])
    keep(c)
    arrive(i_k[3], kx.at[:, 1 - c])
    keep(1 - c)

    grow = 2 * cset // 4
    zper = NZ // 4
    o_g, o_za, o_zn, o_z1, o_z0 = (new_s() for _ in range(5))
    i_za, i_zn, i_z0 = new(), new(), [new(), new()]
    own = jnp.logical_and(diag, y == x)

    def g_rows(rel, yy=None):
        slot = SLOT[rel]
        if yy is None:
            return gout.at[slot * 2 * crow : (slot + 1) * 2 * crow]
        return gout.at[pl.ds(pl.multiple_of((2 * slot + yy) * crow, 16), crow)]

    def z_final(rel, n):
        yy = yh ^ n
        out_sem = o_zn if rel else (o_z0, o_z1)[n]
        j = NEAR.index(rel)
        to = dev(yh_=yy, x_=y, z_=zat(rel), q_=x)
        src = g_rows(rel, yy)
        if rel:
            return copy(out_sem, i_zn, src, zb.at[c, j], to)
        return pltpu.make_async_remote_copy(
            src_ref=src, dst_ref=zb.at[c, j], send_sem=ssem.at[out_sem], recv_sem=rsem.at[i_z0[0] + c],
            device_id=to, device_id_type=MESH,
        )

    def z0_arrive(cc):
        ref = zb.at[cc, 0]
        pltpu.make_async_remote_copy(
            src_ref=ref, dst_ref=ref, send_sem=ssem.at[o_z0], recv_sem=rsem.at[i_z0[0] + cc],
            device_id=d_sib, device_id_type=MESH,
        ).wait_recv()

    def z_relay(rel):
        if rel == HALF:
            for d in range(2):
                rows = pl.ds(d * crow, crow)
                src = gout.at[pl.ds((2 * SLOT[rel] + d) * crow, crow)]
                send(o_za, i_za, src, za.at[6, rows], dev(z_=zat(4 * sign[d])))
            return
        d = 0 if rel > 0 else 1
        hop = abs(rel) - 4
        send(o_za, i_za, g_rows(rel), za.at[2 * (hop - 1) + d], dev(z_=zat(sign[d] * hop)))

    def g_slice(p):
        def total(t, h):
            lo, num = (0, grow) if h is None else (h * (grow // 2), grow // 2)
            return gsum.at[t, pl.ds(p * grow + lo, num)]

        return total

    order = (3, 2, 1, 0)
    g_ring = [scatter(o_g, g_slice(p), g1.at[p], g2.at[p]) for p in range(4)]
    for s in (1, 0):
        for y_ in (y2, yp, ym, y):
            kk = kx[y_, :, s].reshape(4 * hrow, cset)
            gsum[y_, s * cset : (s + 1) * cset] = lax.dot_general(
                kk, fitted[...], (((0,), (0,)), ((), ())), preferred_element_type=F32
            )
        for p in order[2 - 2 * s : 4 - 2 * s]:
            g_ring[p][0]()
    for p in order:
        g_ring[p][1]()
    for p in order:
        gout[p * grow : (p + 1) * grow] = g_ring[p][2]()
        for rel in reversed(REL[p * zper : (p + 1) * zper]):
            if abs(rel) > 4:
                z_relay(rel)
            elif rel and abs(rel) < 4:
                for n in range(2):
                    z_final(rel, n).start()
    z_final(0, 1).start()

    @pl.when(jnp.logical_not(own))
    def _():
        z_final(0, 0).start()

    @pl.when(own)
    def _():
        zb[c, 0] = g_rows(0, yh)[...]

    arrive(i_za, za)
    for d, rel in enumerate((4, -4)):
        ref = g_rows(rel)
        ref[...] = ref[...] + za[d] + za[2 + d] + za[4 + d]
        part = gout.at[pl.ds((2 * SLOT[rel] + d) * crow, crow)]
        part[...] = part[...] + za[6, d * crow : (d + 1) * crow]
        for n in range(2):
            z_final(rel, n).start()

    @pl.when(jnp.logical_not(own))
    def _():
        z0_arrive(c)

    z0_arrive(1 - c)
    arrive(i_zn, zb.at[:, 1:])
    for cc in range(2):
        total = zb[cc, 0]
        for j in range(1, len(NEAR)):
            total = total + zb[cc, j]
        out[:, cc * lab : (cc + 1) * lab] = total * scale

    assert used == [SENDS, ARRIVALS], used
    sent(o_z, cx.at[0 : NZ - 1])
    sent(o_zw, wx.at[0 : NZ - 1])
    sent(o_sc, cx.at[0, 0])
    sent(o_x, px.at[0:6])
    sent(o_sp, px.at[0])
    sent(o_w, wx.at[0:7, 0, 0])
    sent(o_dc, cx)
    sent(o_dr, px.at[0:3])
    sent(o_k, cx.at[0:14])
    sent(o_g, px.at[0:3])
    sent(o_za, za)
    sent(o_zn, zb.at[:, 1:])
    sent(o_z1, zb.at[0, 0])

    @pl.when(jnp.logical_not(diag))
    def _():
        sent(o_w0, wx.at[0, 0, 0])

    @pl.when(jnp.logical_not(own))
    def _():
        sent(o_z0, zb.at[0, 0])


def solution(mesh):
    assert mesh.shape["blk"] == 2 * NX * NZ and mesh.shape["feat"] == 4

    def step(points, centers, coefs):
        rows, qf = points.shape
        crow, labels = coefs.shape
        feats, cset, lab = qf // 2, 2 * HALF * crow, labels // 2
        npts = rows * mesh.shape["blk"]
        nf = qf * mesh.shape["feat"]
        srow, grow, cols = rows // 2 // NY, 2 * cset // 4, cset
        V = pltpu.VMEM
        per_piece = [
            [V(shape(hi - lo), F32) for lo, hi, _ in PIECES]
            for shape in (
                lambda n: (n, 2, rows // 2, cols),
                lambda n: (n, rows // 2, cols),
                lambda n: (2, n // 2, srow, cols),
                lambda n: (2, n, srow, cols),
            )
        ]
        return pl.pallas_call(
            functools.partial(kernel, 1.0 / nf, 1.0 / math.sqrt(npts)),
            out_shape=jax.ShapeDtypeStruct((crow, labels), F32),
            in_specs=[pl.BlockSpec(memory_space=pl.ANY)] * 3,
            out_specs=pl.BlockSpec(memory_space=pltpu.VMEM),
            scratch_shapes=[
                V((2 * NX, 2, rows // 2, feats), BF16),
                V((NZ, 2, crow, feats), BF16),
                V((NZ, NX, 2, crow, lab), BF16),
                V((NX, 2, 2, rows, cset), BF16),
                V((4, 2 * cset, lab), F32),
                V((2 * cset, lab), F32),
                V((2, len(NEAR), crow, lab), F32),
                V((4, 2, grow // 2, lab), F32),
                V((4, 2, grow, lab), F32),
                V((7, 2 * crow, lab), F32),
                V((8 * rows, 1), F32),
                V((2 * rows, lab), BF16),
                *[v for group in per_piece for v in group],
                pltpu.SemaphoreType.DMA((SENDS,)),
                pltpu.SemaphoreType.DMA((ARRIVALS,)),
                pltpu.SemaphoreType.DMA((3,)),
                pltpu.SemaphoreType.REGULAR((2,)),
            ],
            compiler_params=pltpu.CompilerParams(collective_id=0, has_side_effects=True),
        )(points, centers, coefs)

    spec = P("blk", "feat")
    return jax.shard_map(
        step, mesh=mesh, in_specs=(spec, spec, spec), out_specs=spec, check_vma=False
    )
```
